32 devices in a mesh: rows: 8 (over z, y), cols: 4 (over x, core).
Axes of the slice: x: 2, y: 2, z: 4, core: 2. Of those that a mesh axis runs over, the one named last changes fastest.
Arguments:
- token_ids: int32 [32, 256], P('rows'), may hold values from 0 to 8191
- keep_mask: int32 [32, 256], P('rows'), may hold values 0 or 1
- remask_order: int32 [8192], P('rows'), may hold values from 0 to 8191, each once
- embed_table: bfloat16 [8192, 1024], P(None, 'cols'), may hold values from -6 to 6
- mask_embed: bfloat16 [1024], P('cols'), may hold values from -4 to 4
- conv_one: bfloat16 [3, 3, 1024, 1024], P(None, None, None, 'cols'), may hold values from -0.0625 to 0.0625
- gain_one: float32 [1024], P('cols'), may hold values from 0.25 to 1.75
- bias_one: float32 [1024], P('cols'), may hold values from -3 to 3
- conv_two: bfloat16 [3, 3, 1024, 1024], P(None, None, None, 'cols'), may hold values from -0.0625 to 0.0625
- gain_two: float32 [1024], P('cols'), may hold values from 0.25 to 1.75
- bias_two: float32 [1024], P('cols'), may hold values from -3 to 3
- head_weight: bfloat16 [1024, 8192], P(None, 'cols'), may hold values from -15.6 to 15.6
Outputs:
- features: bfloat16 [32, 256, 1024], P('rows', None, 'cols')
- token_logp: float32 [32, 256], P('rows', 'cols')
The draws below stay inside these ranges and needn't reach their ends.
Inputs may be any that keep to these rules, and one draw needn't show every extreme that they name: `remask_order`: each rank appears once.
All inputs are finite; a program needn't handle non-finite values. No bound on the sum of `keep_mask` on one device may be relied on, other than what follows from the above.
Results may differ from the reference program's by a relative error of at most 0.0039.
Values may be sent and summed in bfloat16 or wider, within the bound.
No kernel may reach another device: no remote copies, remote signals or barrier semaphores. Data moves between devices by JAX's collectives and lax.ppermute only.
A program may use at most 128 MiB of HBM per device.

```python
import math
import jax
import jax.numpy as jnp
import numpy as np
from jax import lax

C = 1024
V = 8192
GROUPS = 32
W = 256
H = 32
REMASK = 4096


def draw_head_weight(key, part):
    base_key, shared_key = jax.random.split(jax.random.fold_in(key, 7))
    base = 0.1 * jnp.clip(jax.random.normal(base_key, (C, V), jnp.float32), -6.0, 6.0)
    shared = jnp.clip(jax.random.normal(shared_key, (C, 1), jnp.float32), -4.0, 4.0) * (120.0 / math.sqrt(C))
    return (base + shared).astype(jnp.bfloat16)


def plant(entries, key, least, high):
    index_at = [jax.random.randint(jax.random.fold_in(key, axis), (), 0, length) for axis, length in enumerate(entries.shape)]
    widest = entries.shape.index(max(entries.shape))
    next_to = index_at[:widest] + [(index_at[widest] + 1) % entries.shape[widest]] + index_at[widest + 1:]
    return entries.at[tuple(index_at)].set(least).at[tuple(next_to)].set(high)


def block_levels(key, dims, cuts, smallest, high):
    loudness, own = 1.0, jax.random.fold_in(key, 6)
    for axis_at, blocks in cuts:
        heights = jnp.exp(jax.random.uniform(jax.random.fold_in(own, axis_at), (blocks,), jnp.float32, smallest / len(cuts), high / len(cuts)))
        loudness = loudness * jnp.repeat(heights, dims[axis_at] // blocks).reshape([-1 if axis == axis_at else 1 for axis in range(len(dims))])
    return loudness


def rank_table(number_of, lean):
    loads = [(1 << 20) // math.isqrt(standing ** lean) + 1 for standing in range(1, number_of + 1)]
    scale = 1 + sum(loads) // (1 << 30)
    return np.cumsum(np.array([max(1, weight // scale) for weight in loads]))


def ranked_ids(stream_key, extent, count, slope):
    grid = rank_table(count, slope)
    pick = jax.random.randint(jax.random.fold_in(stream_key, 1), extent, 0, int(grid[count - 1]))
    standing = jnp.searchsorted(jnp.asarray(grid, jnp.int32), pick, side="right")
    return jax.random.permutation(jax.random.fold_in(stream_key, 2), count)[standing].astype(jnp.int32)


def centred(own_key, extent, scale, reach, cuts=(), dtype=jnp.bfloat16):
    level = block_levels(own_key, extent, cuts, -0.22, 0.18) if cuts else 1.0
    array = jax.random.normal(own_key, extent, jnp.float32) * scale * level
    return jnp.minimum(jnp.maximum(array, -reach), reach).astype(dtype)


def setup_inputs(seed: int = 0) -> dict:
    key_of = jax.random.split(jax.random.key(seed), 13)
    return {
        "token_ids": plant(ranked_ids(key_of[0], (H, W), V, 2), jax.random.fold_in(key_of[0], 3), 0, V - 1).astype(jnp.int32),
        "keep_mask": plant((jax.random.randint(key_of[1], (H, W), 0, 4) < 1).astype(jnp.int32), jax.random.fold_in(key_of[1], 1), 0, 1),
        "remask_order": jax.random.permutation(key_of[2], H * W).astype(jnp.int32),
        "embed_table": centred(key_of[3], (V, C), 1.0, 6.0, ((1, 4),)),
        "mask_embed": centred(key_of[4], (C,), 1.0, 4.0, ((0, 4),)),
        "conv_one": centred(key_of[5], (3, 3, C, C), (9 * C) ** -0.5, 0.0625, ((3, 4),)),
        "gain_one": jnp.clip(1.0 + 0.15 * jax.random.normal(key_of[6], (C,), jnp.float32), 0.25, 1.75),
        "bias_one": centred(key_of[7], (C,), 0.5, 3.0, ((0, 4),), jnp.float32),
        "conv_two": centred(key_of[8], (3, 3, C, C), (9 * C) ** -0.5, 0.0625, ((3, 4),)),
        "gain_two": jnp.clip(1.0 + 0.15 * jax.random.normal(key_of[9], (C,), jnp.float32), 0.25, 1.75),
        "bias_two": centred(key_of[10], (C,), 0.5, 3.0, ((0, 4),), jnp.float32),
        "head_weight": draw_head_weight(jax.random.fold_in(key_of[12], 71), 0),
    }


def convolve(field, weight):
    height, width, channels = field.shape
    padded = jnp.pad(field, ((1, 1), (1, 1), (0, 0)))
    total = jnp.zeros((height * width, weight.shape[3]), jnp.float32)
    for shift_row in range(3):
        for shift_col in range(3):
            window = padded[shift_row:shift_row + height, shift_col:shift_col + width].reshape(-1, channels)
            total = total + jnp.dot(window, weight[shift_row, shift_col], preferred_element_type=jnp.float32)
    return total.reshape(height, width, -1)

def group_norm(values, gain, bias):
    height, width, channels = values.shape
    flat = values.reshape(height * width, GROUPS, channels // GROUPS)
    mean = lax.optimization_barrier(jnp.mean(flat, axis=(0, 2)))
    deviation = flat - mean[None, :, None]
    variance = lax.optimization_barrier(jnp.mean(deviation * deviation, axis=(0, 2)))
    normed = deviation / jnp.sqrt(variance + 1e-05)[None, :, None]
    return normed.reshape(height, width, channels) * gain + bias

def reference(token_ids, keep_mask, remask_order, embed_table, mask_embed, conv_one, gain_one, bias_one, conv_two, gain_two, bias_two, head_weight):
    order = remask_order.reshape(token_ids.shape)
    visible = (keep_mask == 1) | (order >= REMASK)
    looked = jnp.take(embed_table, token_ids, axis=0)
    start = jnp.where(visible[:, :, None], looked, mask_embed[None, None, :])
    hidden = jax.nn.silu(group_norm(convolve(start, conv_one), gain_one, bias_one)).astype(jnp.bfloat16)
    second = group_norm(convolve(hidden, conv_two), gain_two, bias_two)
    features = (start.astype(jnp.float32) + second).astype(jnp.bfloat16)

    def row_logp(inputs):
        feature_row, id_row = inputs
        logits = jnp.dot(feature_row, head_weight, preferred_element_type=jnp.float32)
        top = lax.optimization_barrier(jnp.max(logits, axis=1))
        total = jnp.log(lax.optimization_barrier(jnp.sum(jnp.exp(logits - top[:, None]), axis=1))) + top
        picked = jnp.take_along_axis(logits, id_row[:, None].astype(jnp.int32), axis=1)[:, 0]
        return picked - total
    token_logp = lax.map(row_logp, (features, token_ids))
    return (features, token_logp)
```

```python
import jax
import jax.numpy as jnp
from jax import lax
from jax.sharding import PartitionSpec as P

GROUPS = 32
EPS = 1e-05
F32 = jnp.float32
BF16 = jnp.bfloat16


def swap(value):
    n = lax.axis_size("cols")
    return lax.ppermute(value, "cols", [(i, i ^ 1) for i in range(n)])


def cross(value):
    n = lax.axis_size("cols")
    return [
        lax.ppermute(value, "cols", [(i, (i + 2 * s) % n) for i in range(n)])
        for s in range(1, n // 2)
    ]


def sources():
    n = lax.axis_size("cols")
    me = lax.axis_index("cols")
    out = []
    for s in range(n // 2):
        same = lax.rem(me + n - 2 * s, n)
        out += [same, same ^ 1]
    return out


def gathered(value):
    out = [value, swap(value)]
    for far in cross(value):
        out += [far, swap(far)]
    return out


def halo(first, last):
    n = lax.axis_size("rows")
    up = [(i, i + 1) for i in range(n - 1)]
    down = [(i + 1, i) for i in range(n - 1)]
    return lax.ppermute(last, "rows", up), lax.ppermute(first, "rows", down)


def reordered(weight, axis):
    n = lax.axis_size("cols")
    size = weight.shape[axis] // n
    return [lax.dynamic_slice_in_dim(weight, s * size, size, axis) for s in sources()]


def conv(blocks, weights, width):
    count = blocks[0].shape[0] - 2 * width
    parts = []
    for b in range(3):
        total = 0.0
        for x, w in zip(blocks, weights):
            for a in range(3):
                total = total + jnp.dot(
                    x[a * width : a * width + count], w[a, b], preferred_element_type=F32
                )
        parts.append(total)
    col = lax.rem(lax.broadcasted_iota(jnp.int32, (count, 1), 0), width)
    left = jnp.where(col == 0, 0.0, jnp.roll(parts[0], 1, 0))
    right = jnp.where(col == width - 1, 0.0, jnp.roll(parts[2], -1, 0))
    return parts[1] + left + right


def centred(y):
    count, channels = y.shape
    mean = jnp.mean(y, axis=0)
    centre = mean.astype(BF16)
    dev = y - centre.astype(F32)[None]
    spread = jnp.sum(dev * dev, axis=0) - count * (mean - centre.astype(F32)) ** 2
    return dev.astype(BF16), centre, mean, spread


def affine(mean, spread, count, gain, bias, per_group):
    g = mean.reshape(-1, per_group)
    mid = jnp.mean(g, axis=1)
    dev2 = jnp.sum(spread.reshape(-1, per_group) + count * (g - mid[:, None]) ** 2, axis=1)
    population = float(count * per_group)
    state = jnp.stack([mid, dev2])
    n = lax.axis_size("rows")
    step = 1
    while step < n:
        other = lax.ppermute(state, "rows", [(i, i ^ step) for i in range(n)])
        delta = state[0] - other[0]
        state = jnp.stack(
            [
                0.5 * (state[0] + other[0]),
                state[1] + other[1] + delta * delta * (0.5 * population),
            ]
        )
        population *= 2.0
        step *= 2
    rstd = 1.0 / jnp.sqrt(state[1] / population + EPS)
    scale = jnp.repeat(rstd, per_group) * gain
    shift = bias - jnp.repeat(state[0], per_group) * scale
    return jnp.stack([scale, shift])


def local(
    token_ids,
    keep_mask,
    remask_order,
    embed_table,
    mask_embed,
    conv_one,
    gain_one,
    bias_one,
    conv_two,
    gain_two,
    bias_two,
    head_weight,
):
    rows_here, width = token_ids.shape
    n_rows = lax.axis_size("rows")
    num_cols = lax.axis_size("cols")
    height = rows_here * n_rows
    here = gain_one.shape[0]
    channels = here * num_cols
    per_group = channels // GROUPS
    count = rows_here * width
    me_row = lax.axis_index("rows")
    inner_top = me_row > 0
    inner_end = me_row < n_rows - 1

    visible = (keep_mask.reshape(-1) == 1) | (remask_order >= height * width // 2)
    looked = jnp.take(embed_table, token_ids.reshape(-1), axis=0, mode="clip")
    start = jnp.where(visible[:, None], looked, mask_embed[None, :])

    start_blocks = gathered(start)
    edge = [halo(s[:width], s[count - width :]) for s in start_blocks[::2]]
    edges = []
    for before, after in edge:
        edges += [(before, after), (swap(before), swap(after))]
    field = [
        jnp.concatenate([b, s, a], axis=0) for s, (b, a) in zip(start_blocks, edges)
    ]
    w_one = reordered(conv_one, 2)
    w_two = reordered(conv_two, 2)
    w_head = reordered(head_weight, 0)
    y_one = conv(field, w_one, width)

    dev, centre, mean, spread = centred(y_one)
    packed = jnp.concatenate([dev, jnp.broadcast_to(centre[None], (16, here))], axis=0)
    blocks = gathered(packed)
    edges = []
    for s in blocks[::2]:
        c = s[count:]
        before, after = halo(
            jnp.concatenate([s[:width], c]), jnp.concatenate([s[count - width : count], c])
        )
        edges += [(before, after), (swap(before), swap(after))]
    norms = gathered(affine(mean, spread, count, gain_one, bias_one, per_group))

    def act(part, norm, keep):
        body, mid = part[:-16], part[-16].astype(F32)
        v = body.astype(F32) * norm[0][None] + (mid * norm[0] + norm[1])[None]
        v = v / (1.0 + jnp.exp(-v))
        if keep is not None:
            v = jnp.where(keep, v, 0.0)
        return v.astype(BF16)

    hidden = [
        jnp.concatenate([act(b, m, inner_top), act(s, m, None), act(a, m, inner_end)], axis=0)
        for s, (b, a), m in zip(blocks, edges, norms)
    ]
    y_two = conv(hidden, w_two, width)

    dev, centre, mean, spread = centred(y_two)
    packed = jnp.concatenate([dev, jnp.broadcast_to(centre[None], (16, here))], axis=0)
    blocks = gathered(packed)
    norm_two = affine(mean, spread, count, gain_two, bias_two, per_group)
    norms = gathered(norm_two)
    features = (start.astype(F32) + (y_two * norm_two[0][None] + norm_two[1][None])).astype(BF16)
    logits = 0.0
    for s, part, m, w in zip(start_blocks, blocks, norms, w_head):
        mid = part[-16].astype(F32)
        feat = part[:count].astype(F32) * m[0][None] + (mid * m[0] + m[1])[None]
        feat = (s.astype(F32) + feat).astype(BF16)
        logits = logits + jnp.dot(feat, w, preferred_element_type=F32)
    vocab_here = head_weight.shape[1]
    top = jnp.max(logits, axis=1)
    summed = jnp.sum(jnp.exp(logits - top[:, None]), axis=1)
    offset = lax.axis_index("cols") * vocab_here
    vocab_ids = lax.broadcasted_iota(jnp.int32, (1, vocab_here), 1) + offset
    hits = vocab_ids == token_ids.reshape(-1, 1)
    picked = jnp.sum(jnp.where(hits, logits, 0.0), axis=1)
    state = jnp.stack([top, summed, picked])
    step = 1
    while step < num_cols:
        other = lax.ppermute(state, "cols", [(i, i ^ step) for i in range(num_cols)])
        high = jnp.maximum(state[0], other[0])
        total = state[1] * jnp.exp(state[0] - high) + other[1] * jnp.exp(other[0] - high)
        state = jnp.stack([high, total, state[2] + other[2]])
        step *= 2
    logp = (state[2] - state[0] - jnp.log(state[1])).reshape(rows_here, width)
    slice_width = width // num_cols
    token_logp = lax.dynamic_slice_in_dim(
        logp, lax.axis_index("cols") * slice_width, slice_width, 1
    )
    return (features.reshape(rows_here, width, here), token_logp)


def solution(mesh):
    in_specs = (
        P("rows", None),
        P("rows", None),
        P("rows"),
        P(None, "cols"),
        P("cols"),
        P(None, None, None, "cols"),
        P("cols"),
        P("cols"),
        P(None, None, None, "cols"),
        P("cols"),
        P("cols"),
        P(None, "cols"),
    )
    out_specs = (P("rows", None, "cols"), P("rows", "cols"))
    return jax.shard_map(local, mesh=mesh, in_specs=in_specs, out_specs=out_specs, check_vma=False)
```

```python
import jax
import jax.numpy as jnp
from jax import lax
from jax.experimental import pallas as pl
from jax.experimental.pallas import tpu as pltpu
from jax.sharding import PartitionSpec as P

GROUPS = 32
EPS = 1e-05
PAD = 16
F32 = jnp.float32
BF16 = jnp.bfloat16
VMEM = pl.BlockSpec(memory_space=pltpu.VMEM)
SMEM = pl.BlockSpec(memory_space=pltpu.SMEM)


def swap(value):
    n = lax.axis_size("cols")
    return lax.ppermute(value, "cols", [(i, i ^ 1) for i in range(n)])


def cross(value):
    n = lax.axis_size("cols")
    return [
        lax.ppermute(value, "cols", [(i, (i + 2 * s) % n) for i in range(n)])
        for s in range(1, n // 2)
    ]


def sources():
    n = lax.axis_size("cols")
    me = lax.axis_index("cols")
    out = []
    for s in range(n // 2):
        same = lax.rem(me + n - 2 * s, n)
        out += [same, same ^ 1]
    return out


def gathered(value):
    out = [value, swap(value)]
    for far in cross(value):
        out += [far, swap(far)]
    return out


def upward(value):
    n = lax.axis_size("rows")
    return lax.ppermute(value, "rows", [(i, i + 1) for i in range(n - 1)])


def downward(value):
    n = lax.axis_size("rows")
    return lax.ppermute(value, "rows", [(i + 1, i) for i in range(n - 1)])


def tile_sum(value):
    return jnp.sum(value, axis=0, keepdims=True)


def taps(src, fields, w, b, i, first, total):
    here = w.shape[3]
    for k, field in enumerate(fields):
        at = pl.multiple_of(src[first + k] * here, here)
        for a in range(3):
            part = jnp.dot(field(a + i), w[a, b, pl.ds(at, here), :], preferred_element_type=F32)
            total = part if total is None else total + part
    return total


def finish(parts, y_ref, packed_ref, stats_ref, rows, width, per_group):
    here = y_ref.shape[1]
    count = rows * width
    col = lax.broadcasted_iota(jnp.int32, (width, here), 0)
    total = jnp.zeros((1, here), F32)
    for i in range(rows):
        left = jnp.where(col == 0, 0.0, pltpu.roll(parts[0, i], 1, 0))
        right = jnp.where(col == width - 1, 0.0, pltpu.roll(parts[2, i], width - 1, 0))
        y = parts[1, i] + left + right
        y_ref[i * width : (i + 1) * width, :] = y
        total = total + tile_sum(y)
    mean = total / count
    centre = mean.astype(BF16).astype(F32)
    square = jnp.zeros((1, here), F32)
    for i in range(rows):
        dev = y_ref[i * width : (i + 1) * width, :] - centre
        packed_ref[i * width : (i + 1) * width, :] = dev.astype(BF16)
        square = square + tile_sum(dev * dev)
    packed_ref[count : count + PAD, :] = jnp.broadcast_to(centre, (PAD, here)).astype(BF16)
    spread = square - count * (mean - centre) * (mean - centre)
    same = (
        lax.broadcasted_iota(jnp.int32, (here, here), 0) // per_group
        == lax.broadcasted_iota(jnp.int32, (here, here), 1) // per_group
    ).astype(F32)

    def over_group(value):
        return jnp.dot(
            jnp.broadcast_to(value, (8, here)),
            same,
            precision=lax.Precision.HIGHEST,
            preferred_element_type=F32,
        )

    mid = over_group(mean) / per_group
    away = mean - mid[:1]
    stats_ref[0] = mid
    stats_ref[1] = over_group(spread + count * away * away)


def first_half(rows, width, src, *refs):
    fields, w, parts = refs[:-2], refs[-2], refs[-1]
    fields = [row_reader(fields[3 * k : 3 * k + 3], rows, width) for k in range(len(fields) // 3)]
    for b in range(3):
        for i in range(rows):
            parts[b, i] = taps(src, fields, w, b, i, 0, None)


def row_reader(refs, rows, width):
    main, before, after = refs

    def read(r):
        if r == 0:
            return before[0:width, :]
        if r == rows + 1:
            return after[0:width, :]
        return main[(r - 1) * width : r * width, :]

    return read


def second_half(rows, width, per_group, first, src, *refs):
    fields, (w, before, packed, stats, parts, y) = refs[:-6], refs[-6:]
    fields = [row_reader(fields[3 * k : 3 * k + 3], rows, width) for k in range(len(fields) // 3)]
    for b in range(3):
        for i in range(rows):
            parts[b, i] = taps(src, fields, w, b, i, first, before[b, i])
    finish(parts, y, packed, stats, rows, width, per_group)


def second_conv(rows, width, per_group, n, src, flags, *refs):
    fields, norms = refs[: 3 * n], refs[3 * n : 4 * n]
    w, y, packed, stats, parts, hidden = refs[4 * n :]
    for k in range(n):
        main, before, after = fields[3 * k : 3 * k + 3]
        scale = norms[k][0][:1]
        shift = norms[k][1][:1]
        for r in range(rows + 2):
            ref = before if r == 0 else after if r == rows + 1 else main
            base = 0 if r in (0, rows + 1) else (r - 1) * width
            mid_at = ref.shape[0] - PAD
            mid = ref[mid_at : mid_at + PAD, :].astype(F32)[:1]
            v = ref[base : base + width, :].astype(F32) * scale + (mid * scale + shift)
            v = v * (0.5 + 0.5 * jnp.tanh(0.5 * v))
            if r == 0:
                v = jnp.where(flags[0] > 0, v, 0.0)
            if r == rows + 1:
                v = jnp.where(flags[1] > 0, v, 0.0)
            hidden[k, r * width : (r + 1) * width, :] = v.astype(BF16)
    readers = [
        (lambda r, k=k: hidden[k, r * width : (r + 1) * width, :]) for k in range(n)
    ]
    for b in range(3):
        for i in range(rows):
            parts[b, i] = taps(src, readers, w, b, i, 0, None)
    finish(parts, y, packed, stats, rows, width, per_group)


def head(count, n, tile, src, *refs):
    starts, devs, norms = refs[:n], refs[n : 2 * n], refs[2 * n : 3 * n]
    w, ids, out, feat, logits, top, summed, picked = refs[3 * n :]
    here = starts[0].shape[1]
    step = 256
    tiles = w.shape[1] // tile
    for k in range(n):
        scale = norms[k][0][:1]
        mid = devs[k][count : count + PAD, :].astype(F32)[:1]
        shift = mid * scale + norms[k][1][:1]
        for r in range(0, count, step):
            value = devs[k][r : r + step, :].astype(F32) * scale + shift
            feat[k, r : r + step, :] = (starts[k][r : r + step, :].astype(F32) + value).astype(BF16)
    top[...] = jnp.full(top.shape, -jnp.inf, F32)
    summed[...] = jnp.zeros(summed.shape, F32)
    picked[...] = jnp.zeros(picked.shape, F32)

    def multiply(t, slot):
        total = None
        for k in range(n):
            at = pl.multiple_of(src[k] * here, here)
            part = jnp.dot(
                feat[k],
                w[pl.ds(at, here), pl.ds(pl.multiple_of(t * tile, tile), tile)],
                preferred_element_type=F32,
            )
            total = part if total is None else total + part
        logits[slot] = total

    def reduce(t, slot):
        for r in range(0, count, 64):
            rows = slice(r, r + 64)
            pieces = [logits[slot, rows, g : g + 128] for g in range(0, tile, 128)]
            old = top[rows, :]
            new = old
            for piece in pieces:
                new = jnp.maximum(new, piece)
            total = summed[rows, :] * jnp.exp(old - new)
            hit = picked[rows, :]
            rel = ids[rows, :] - t * tile
            for g, piece in enumerate(pieces):
                total = total + jnp.exp(piece - new)
                hit = jnp.where(rel == g * 128, piece, hit)
            top[rows, :] = new
            summed[rows, :] = total
            picked[rows, :] = hit

    multiply(0, 0)

    def body(t, carry):
        multiply(t, lax.rem(t, 2))
        reduce(t - 1, lax.rem(t + 1, 2))
        return carry

    lax.fori_loop(1, tiles, body, 0)
    reduce(tiles - 1, (tiles - 1) % 2)
    lane = lax.broadcasted_iota(jnp.int32, (128, 128), 1)
    for r in range(0, count, 128):
        rows = slice(r, r + 128)
        high = jnp.max(top[rows, :], axis=1, keepdims=True)
        total = jnp.sum(summed[rows, :] * jnp.exp(top[rows, :] - high), axis=1, keepdims=True)
        hit = jnp.sum(picked[rows, :], axis=1, keepdims=True)
        stacked = jnp.where(lane == 0, high, jnp.where(lane == 1, total, hit))
        out[:, rows] = jnp.transpose(stacked)[:8]


def params(mib):
    return pltpu.CompilerParams(vmem_limit_bytes=mib << 20)


def over_rows(stats, count, per_group, gain, bias):
    population = float(count * per_group)
    n = lax.axis_size("rows")
    step = 1
    while step < n:
        other = lax.ppermute(stats, "rows", [(i, i ^ step) for i in range(n)])
        delta = stats[0] - other[0]
        stats = jnp.stack(
            [
                0.5 * (stats[0] + other[0]),
                stats[1] + other[1] + delta * delta * (0.5 * population),
            ]
        )
        population *= 2.0
        step *= 2
    scale = gain[None, :] / jnp.sqrt(stats[1] / population + EPS)
    return jnp.stack([scale, bias[None, :] - stats[0] * scale])


def local(
    token_ids,
    keep_mask,
    remask_order,
    embed_table,
    mask_embed,
    conv_one,
    gain_one,
    bias_one,
    conv_two,
    gain_two,
    bias_two,
    head_weight,
):
    rows, width = token_ids.shape
    n_rows = lax.axis_size("rows")
    n = lax.axis_size("cols")
    height = rows * n_rows
    here = gain_one.shape[0]
    per_group = here * n // GROUPS
    count = rows * width
    me_row = lax.axis_index("rows")
    flags = jnp.stack([me_row > 0, me_row < n_rows - 1]).astype(jnp.int32)
    src = jnp.stack(sources()).astype(jnp.int32)

    visible = (keep_mask.reshape(-1) == 1) | (remask_order >= height * width // 2)
    looked = jnp.take(embed_table, token_ids.reshape(-1), axis=0, mode="clip")
    start = jnp.where(visible[:, None], looked, mask_embed[None, :])

    starts = gathered(start)
    fields = []
    for s in starts[::2]:
        before, after = upward(s[count - width :]), downward(s[:width])
        fields += [(before, after), (swap(before), swap(after))]
    fields = [(s, b, a) for s, (b, a) in zip(starts, fields)]

    packed_shape = jax.ShapeDtypeStruct((count + PAD, here), BF16)
    stats_shape = jax.ShapeDtypeStruct((2, 8, here), F32)
    parts_shape = (3, rows, width, here)
    y_shape = (count, here)
    partial_one = pl.pallas_call(
        lambda *refs: first_half(rows, width, *refs),
        out_shape=jax.ShapeDtypeStruct(parts_shape, F32),
        in_specs=[SMEM] + [VMEM] * 7,
        out_specs=VMEM,
        compiler_params=params(32),
        name="conv_one_near",
    )(src, *fields[0], *fields[1], conv_one)
    far = [f for three in fields[2:] for f in three]
    packed, stats = pl.pallas_call(
        lambda *refs: second_half(rows, width, per_group, 2, *refs),
        out_shape=(packed_shape, stats_shape),
        in_specs=[SMEM] + [VMEM] * (len(far) + 2),
        out_specs=(VMEM, VMEM),
        scratch_shapes=[pltpu.VMEM(parts_shape, F32), pltpu.VMEM(y_shape, F32)],
        compiler_params=params(32),
        name="conv_one_far",
    )(src, *far, conv_one, partial_one)

    blocks = gathered(packed)
    fields = []
    for s in blocks[::2]:
        c = s[count:]
        before = upward(jnp.concatenate([s[count - width : count], c]))
        after = downward(jnp.concatenate([s[:width], c]))
        fields += [(before, after), (swap(before), swap(after))]
    fields = [f for s, (b, a) in zip(blocks, fields) for f in (s, b, a)]
    norms = gathered(over_rows(stats, count, per_group, gain_one, bias_one))
    y_two, packed, stats = pl.pallas_call(
        lambda *refs: second_conv(rows, width, per_group, n, *refs),
        out_shape=(jax.ShapeDtypeStruct(y_shape, F32), packed_shape, stats_shape),
        in_specs=[SMEM, SMEM] + [VMEM] * (4 * n + 1),
        out_specs=(VMEM, VMEM, VMEM),
        scratch_shapes=[
            pltpu.VMEM(parts_shape, F32),
            pltpu.VMEM((n, count + 2 * width, here), BF16),
        ],
        compiler_params=params(32),
        name="conv_two",
    )(src, flags, *fields, *norms, conv_two)

    blocks = gathered(packed)
    norm_two = over_rows(stats, count, per_group, gain_two, bias_two)
    norms = gathered(norm_two)
    features = start.astype(F32) + (y_two * norm_two[0, :1] + norm_two[1, :1])
    features = features.astype(BF16).reshape(rows, width, here)

    vocab_here = head_weight.shape[1]
    ids = token_ids.reshape(-1, 1) - lax.axis_index("cols") * vocab_here
    ids = ids - lax.broadcasted_iota(jnp.int32, (1, 128), 1)
    tile = min(512, vocab_here)
    state = pl.pallas_call(
        lambda *refs: head(count, n, tile, *refs),
        out_shape=jax.ShapeDtypeStruct((8, count), F32),
        in_specs=[SMEM] + [VMEM] * (3 * n + 2),
        out_specs=VMEM,
        scratch_shapes=[
            pltpu.VMEM((n, count, here), BF16),
            pltpu.VMEM((2, count, tile), F32),
            pltpu.VMEM((count, 128), F32),
            pltpu.VMEM((count, 128), F32),
            pltpu.VMEM((count, 128), F32),
        ],
        compiler_params=params(32),
        name="head",
    )(src, *starts, *blocks, *norms, head_weight, ids)
    step = 1
    while step < n:
        other = lax.ppermute(state, "cols", [(i, i ^ step) for i in range(n)])
        high = jnp.maximum(state[0], other[0])
        total = state[1] * jnp.exp(state[0] - high) + other[1] * jnp.exp(other[0] - high)
        state = jnp.stack([high, total, state[2] + other[2]])
        step *= 2
    logp = (state[2] - state[0] - jnp.log(state[1])).reshape(rows, width)
    slice_width = width // n
    token_logp = lax.dynamic_slice_in_dim(
        logp, lax.axis_index("cols") * slice_width, slice_width, 1
    )
    return (features, token_logp)


def solution(mesh):
    in_specs = (
        P("rows", None),
        P("rows", None),
        P("rows"),
        P(None, "cols"),
        P("cols"),
        P(None, None, None, "cols"),
        P("cols"),
        P("cols"),
        P(None, None, None, "cols"),
        P("cols"),
        P("cols"),
        P(None, "cols"),
    )
    out_specs = (P("rows", None, "cols"), P("rows", "cols"))
    return jax.shard_map(local, mesh=mesh, in_specs=in_specs, out_specs=out_specs, check_vma=False)
```

```python
import jax
import jax.numpy as jnp
from jax import lax
from jax.experimental import pallas as pl
from jax.experimental.pallas import tpu as pltpu
from jax.sharding import PartitionSpec as P


GROUPS = 32
EPS = 1e-05
PAD = 16
F32 = jnp.float32
BF16 = jnp.bfloat16
VMEM = pl.BlockSpec(memory_space=pltpu.VMEM)
SMEM = pl.BlockSpec(memory_space=pltpu.SMEM)
HBM = pl.BlockSpec(memory_space=pltpu.HBM)


def swap(value):
    n = lax.axis_size("cols")
    return lax.ppermute(value, "cols", [(i, i ^ 1) for i in range(n)])


def cross(value):
    n = lax.axis_size("cols")
    return [
        lax.ppermute(value, "cols", [(i, (i + 2 * s) % n) for i in range(n)])
        for s in range(1, n // 2)
    ]


def sources():
    n = lax.axis_size("cols")
    me = lax.axis_index("cols")
    out = []
    for s in range(n // 2):
        same = lax.rem(me + n - 2 * s, n)
        out += [same, same ^ 1]
    return out


def gathered(value, after=None):
    out = [value, swap(value)]
    for far in cross(value):
        if after is not None:
            far, _ = lax.optimization_barrier((far, after))
        out += [far, swap(far)]
    return out


def far_blocks(values, after):
    out = []
    for far in values:
        far, _ = lax.optimization_barrier((far, after))
        out += [far, swap(far)]
    return out


def upward(value):
    n = lax.axis_size("rows")
    return lax.ppermute(value, "rows", [(i, i + 1) for i in range(n - 1)])


def downward(value):
    n = lax.axis_size("rows")
    return lax.ppermute(value, "rows", [(i + 1, i) for i in range(n - 1)])


def tile_sum(value):
    return jnp.sum(value, axis=0, keepdims=True)


def load_taps(src, first, w, held, sems):
    here = w.shape[3]
    copies = []
    for b in range(3):
        for k in range(held.shape[0]):
            at = pl.multiple_of(src[first + k] * here, here)
            copy = pltpu.make_async_copy(
                w.at[:, b, pl.ds(at, here), :], held.at[k, b], sems.at[b, k]
            )
            copy.start()
            copies.append(copy)
    return copies


def taps(fields, held, b, i, total):
    for k, field in enumerate(fields):
        for a in range(3):
            part = jnp.dot(field(a + i), held[k, b, a], preferred_element_type=F32)
            total = part if total is None else total + part
    return total


def joined_taps(before, here, after):
    width = here.shape[0]
    col = lax.broadcasted_iota(jnp.int32, here.shape, 0)
    left = jnp.where(col == 0, 0.0, pltpu.roll(before, 1, 0))
    right = jnp.where(col == width - 1, 0.0, pltpu.roll(after, width - 1, 0))
    return here + left + right


def finish(parts, y_ref, packed_ref, stats_ref, rows, width, per_group):
    here = y_ref.shape[1]
    count = rows * width
    total = jnp.zeros((1, here), F32)
    for i in range(rows):
        y = joined_taps(parts[0, i], parts[1, i], parts[2, i])
        y_ref[i * width : (i + 1) * width, :] = y
        total = total + tile_sum(y)
    mean = total / count
    centre = mean.astype(BF16).astype(F32)
    square = jnp.zeros((1, here), F32)
    for i in range(rows):
        dev = y_ref[i * width : (i + 1) * width, :] - centre
        packed_ref[i * width : (i + 1) * width, :] = dev.astype(BF16)
        square = square + tile_sum(dev * dev)
    packed_ref[count : count + PAD, :] = jnp.broadcast_to(centre, (PAD, here)).astype(BF16)
    spread = square - count * (mean - centre) * (mean - centre)
    same = (
        lax.broadcasted_iota(jnp.int32, (here, here), 0) // per_group
        == lax.broadcasted_iota(jnp.int32, (here, here), 1) // per_group
    ).astype(F32)

    def over_group(value):
        return jnp.dot(
            jnp.broadcast_to(value, (8, here)),
            same,
            precision=lax.Precision.HIGHEST,
            preferred_element_type=F32,
        )

    mid = over_group(mean) / per_group
    away = mean - mid[:1]
    stats_ref[0] = mid
    stats_ref[1] = over_group(spread + count * away * away)


def reader(rows, width, main, inner, outer=None):
    def read(r):
        if r == 0:
            return outer[0:width, :]
        if r == 1:
            return inner[0:width, :]
        if r == rows + 2:
            return inner[width : 2 * width, :]
        if r == rows + 3:
            return outer[width : 2 * width, :]
        return main[(r - 2) * width : (r - 1) * width, :]

    return read


def conv_near(rows, width, src, *refs):
    fields, (w, parts, far, held, sems, far_sems) = refs[:6], refs[6:]
    copies = load_taps(src, 0, w, held, sems)
    later = load_taps(src, 2, w, far, far_sems)
    readers = [reader(rows, width, *fields[3 * k : 3 * k + 3]) for k in range(2)]
    for b in range(3):
        for copy in copies[2 * b : 2 * b + 2]:
            copy.wait()
        for i in range(rows + 2):
            parts[b, i] = taps(readers, held, b, i, None)
    for copy in later:
        copy.wait()


def fetch_taps(src, w, held, sems):
    for copy in load_taps(src, 0, w, held, sems):
        copy.wait()


def fetch_head(src, w, held, sems):
    n, here = held.shape[0], held.shape[1]
    copies = []
    for k in range(n):
        at = pl.multiple_of(src[k] * here, here)
        copies.append(pltpu.make_async_copy(w.at[pl.ds(at, here), :], held.at[k], sems.at[k]))
        copies[-1].start()
    for copy in copies:
        copy.wait()


def conv_far(rows, width, per_group, *refs):
    fields, (held, before, packed, stats, parts, y) = refs[:-6], refs[-6:]
    readers = [reader(rows, width, *fields[k : k + 2]) for k in range(0, len(fields), 2)]
    for b in range(3):
        for i in range(rows):
            parts[b, i] = taps(readers, held, b, i + 1, before[b, i + 1])
    finish(parts, y, packed, stats, rows, width, per_group)


def conv_edge(rows, width, *refs):
    fields, (held, before, packed, out) = refs[:-4], refs[-4:]
    readers = [reader(rows, width, *fields[k : k + 3]) for k in range(0, len(fields), 3)]
    count = rows * width
    centre = packed[count : count + PAD, :].astype(F32)[:1]
    for j, i in enumerate((0, rows + 1)):
        y = joined_taps(*[taps(readers, held, b, i, before[b, i]) for b in range(3)])
        out[j * width : (j + 1) * width, :] = (y - centre).astype(BF16)


def activated(rows, width, flags, fields, norms, hidden):
    count = rows * width
    for k in range(len(norms)):
        main, edge = fields[2 * k : 2 * k + 2]
        scale = norms[k][0][:1]
        mid = main[count : count + PAD, :].astype(F32)[:1]
        shift = mid * scale + norms[k][1][:1]
        for r in range(rows + 2):
            if r == 0:
                v = edge[0:width, :]
            elif r == rows + 1:
                v = edge[width : 2 * width, :]
            else:
                v = main[(r - 1) * width : r * width, :]
            v = v.astype(F32) * scale + shift
            v = v * (0.5 + 0.5 * jnp.tanh(0.5 * v))
            if r == 0:
                v = jnp.where(flags[0] > 0, v, 0.0)
            if r == rows + 1:
                v = jnp.where(flags[1] > 0, v, 0.0)
            hidden[k, r * width : (r + 1) * width, :] = v.astype(BF16)
    return [
        (lambda r, k=k: hidden[k, r * width : (r + 1) * width, :]) for k in range(len(norms))
    ]


def second_near(rows, width, flags, *refs):
    fields, norms, (held, parts, hidden) = refs[:4], refs[4:6], refs[6:]
    readers = activated(rows, width, flags, fields, norms, hidden)
    for b in range(3):
        for i in range(rows):
            parts[b, i] = taps(readers, held, b, i, None)


def second_far(rows, width, per_group, n, flags, *refs):
    fields, norms = refs[: 2 * n], refs[2 * n : 3 * n]
    held, near, y, packed, stats, parts, hidden = refs[3 * n :]
    held = held.at[2:]
    readers = activated(rows, width, flags, fields, norms, hidden)
    for b in range(3):
        for i in range(rows):
            parts[b, i] = taps(readers, held, b, i, near[b, i])
    finish(parts, y, packed, stats, rows, width, per_group)


def head(count, n, tile, *refs):
    starts, devs, norms = refs[:n], refs[n : 2 * n], refs[2 * n : 3 * n]
    held, ids, out, feat, logits, top, summed, picked = refs[3 * n :]
    step = 256
    tiles = held.shape[2] // tile
    for k in range(n):
        scale = norms[k][0][:1]
        mid = devs[k][count : count + PAD, :].astype(F32)[:1]
        shift = mid * scale + norms[k][1][:1]
        for r in range(0, count, step):
            value = devs[k][r : r + step, :].astype(F32) * scale + shift
            feat[k, r : r + step, :] = (starts[k][r : r + step, :].astype(F32) + value).astype(BF16)
    top[...] = jnp.full(top.shape, -jnp.inf, F32)
    summed[...] = jnp.zeros(summed.shape, F32)
    picked[...] = jnp.zeros(picked.shape, F32)

    def multiply(t, slot):
        total = None
        for k in range(n):
            part = jnp.dot(
                feat[k],
                held[k, :, pl.ds(pl.multiple_of(t * tile, tile), tile)],
                preferred_element_type=F32,
            )
            total = part if total is None else total + part
        logits[slot] = total

    def reduce(t, slot):
        for r in range(0, count, 64):
            rows = slice(r, r + 64)
            pieces = [logits[slot, rows, g : g + 128] for g in range(0, tile, 128)]
            old = top[rows, :]
            new = old
            for piece in pieces:
                new = jnp.maximum(new, piece)
            total = summed[rows, :] * jnp.exp(old - new)
            hit = picked[rows, :]
            rel = ids[rows, :] - t * tile
            for g, piece in enumerate(pieces):
                total = total + jnp.exp(piece - new)
                hit = jnp.where(rel == g * 128, piece, hit)
            top[rows, :] = new
            summed[rows, :] = total
            picked[rows, :] = hit

    multiply(0, 0)

    def body(t, carry):
        multiply(t, lax.rem(t, 2))
        reduce(t - 1, lax.rem(t + 1, 2))
        return carry

    lax.fori_loop(1, tiles, body, 0)
    reduce(tiles - 1, (tiles - 1) % 2)
    lane = lax.broadcasted_iota(jnp.int32, (128, 128), 1)
    for r in range(0, count, 128):
        rows = slice(r, r + 128)
        high = jnp.max(top[rows, :], axis=1, keepdims=True)
        total = jnp.sum(summed[rows, :] * jnp.exp(top[rows, :] - high), axis=1, keepdims=True)
        hit = jnp.sum(picked[rows, :], axis=1, keepdims=True)
        stacked = jnp.where(lane == 0, high, jnp.where(lane == 1, total, hit))
        out[:, rows] = jnp.transpose(stacked)[:8]


def in_hbm(value):
    return pltpu.with_memory_space_constraint(value, pltpu.HBM)


def params(mib):
    return pltpu.CompilerParams(vmem_limit_bytes=mib << 20)


def over_rows(stats, count, per_group, gains, biases, between=None):
    stats = jnp.stack([stats] + cross(stats))
    population = float(count * per_group)
    n = lax.axis_size("rows")
    step = 1
    while step < n:
        radix = 4 if step > 1 and n // step % 4 == 0 else 2
        others = []
        for j in range(1, radix):
            move = [(i, i ^ (step * j)) for i in range(n)]
            others.append(lax.ppermute(stats, "rows", move))
        states = [stats] + others
        mid = sum(t[:, 0] for t in states) / radix
        away = sum((t[:, 0] - mid) * (t[:, 0] - mid) for t in states)
        stats = jnp.stack([mid, sum(t[:, 1] for t in states) + population * away], axis=1)
        population *= radix
        step *= radix
        if between is not None:
            between(stats)
            between = None
    scale = gains / jnp.sqrt(stats[:, 1] / population + EPS)
    mine = jnp.stack([scale, biases - stats[:, 0] * scale], axis=1)
    other = swap(mine)
    return [f for k in range(mine.shape[0]) for f in (mine[k], other[k])]


def step_of(
    token_ids,
    keep_mask,
    remask_order,
    embed_table,
    mask_embed,
    conv_one,
    gain_one,
    bias_one,
    conv_two,
    gain_two,
    bias_two,
    head_weight,
):
    rows, width = token_ids.shape
    n_rows = lax.axis_size("rows")
    n = lax.axis_size("cols")
    height = rows * n_rows
    here = gain_one.shape[0]
    per_group = here * n // GROUPS
    count = rows * width
    me_row = lax.axis_index("rows")
    flags = jnp.stack([me_row > 0, me_row < n_rows - 1]).astype(jnp.int32)
    src = jnp.stack(sources()).astype(jnp.int32)

    def look(codes):
        rows_of = jnp.take(embed_table, jnp.maximum(codes - 2, 0), axis=0, mode="clip")
        rows_of = jnp.where(codes[:, None] == 1, mask_embed[None, :], rows_of)
        return jnp.where(codes[:, None] == 0, 0, rows_of)

    looked = jnp.take(embed_table, token_ids.reshape(-1), axis=0, mode="clip")
    main_far = cross(looked)
    token_ids, keep_mask, remask_order, looked = lax.optimization_barrier(
        (token_ids, keep_mask, remask_order, looked)
    )
    visible = (keep_mask.reshape(-1) == 1) | (remask_order >= height * width // 2)
    code = jnp.where(visible, token_ids.reshape(-1) + 2, 1)
    start = jnp.where(visible[:, None], looked, mask_embed[None, :])
    above, below = upward(code[count - 2 * width :]), downward(code[: 2 * width])
    halo = look(
        jnp.concatenate([above[width:], below[:width], above[:width], below[width:]])
    )
    inner, outer = halo[: 2 * width], halo[2 * width :]
    mains = [start, swap(start)]
    inners, inner_far = [inner, swap(inner)], cross(inner)
    outers, outer_far = [outer, swap(outer)], cross(outer)

    packed_shape = jax.ShapeDtypeStruct((count + PAD, here), BF16)
    stats_shape = jax.ShapeDtypeStruct((2, 8, here), F32)
    parts_shape = (3, rows, width, here)
    y_shape = (count, here)
    own = jnp.stack([gain_one, bias_one, gain_two, bias_two, mask_embed.astype(F32)])
    own = jnp.broadcast_to(own[:, None], (5, 8, here))
    affine = jnp.stack([own] + cross(own))
    mask_far = affine[1:, 4, 0].astype(BF16)
    main_far = [
        jnp.where(visible[:, None], far, mask_far[k]) for k, far in enumerate(main_far)
    ]
    fields = [f for k in range(2) for f in (mains[k], inners[k], outers[k])]
    vocab_here = head_weight.shape[1]
    near, taps_far = pl.pallas_call(
        lambda *refs: conv_near(rows, width, *refs),
        out_shape=(
            jax.ShapeDtypeStruct((3, rows + 2, width, here), F32),
            jax.ShapeDtypeStruct((n - 2, 3, 3, here, here), BF16),
        ),
        in_specs=[SMEM] + [VMEM] * 6 + [HBM],
        out_specs=(VMEM,) * 2,
        scratch_shapes=[
            pltpu.VMEM((2, 3, 3, here, here), BF16),
            pltpu.SemaphoreType.DMA((3, 2)),
            pltpu.SemaphoreType.DMA((3, n - 2)),
        ],
        compiler_params=params(12),
        name="conv_near",
    )(src, *fields, in_hbm(conv_one))
    mains += far_blocks(main_far, near)
    inners += far_blocks(inner_far, near)
    outers += far_blocks(outer_far, near)
    fields = [f for k in range(2, n) for f in (mains[k], inners[k])]
    packed, stats = pl.pallas_call(
        lambda *refs: conv_far(rows, width, per_group, *refs),
        out_shape=(packed_shape, stats_shape),
        in_specs=[VMEM] * (len(fields) + 2),
        out_specs=(VMEM, VMEM),
        scratch_shapes=[pltpu.VMEM(parts_shape, F32), pltpu.VMEM(y_shape, F32)],
        compiler_params=params(12),
        name="conv_far",
    )(*fields, taps_far, near)
    fields = [f for k in range(2, n) for f in (mains[k], inners[k], outers[k])]
    edge_box = []

    def make_edge(state):
        centre, _ = lax.optimization_barrier((packed, state))
        edge_box.append(
            pl.pallas_call(
                lambda *refs: conv_edge(rows, width, *refs),
                out_shape=jax.ShapeDtypeStruct((2 * width, here), BF16),
                in_specs=[VMEM] * (len(fields) + 3),
                out_specs=VMEM,
                compiler_params=params(8),
                name="conv_edge",
            )(*fields, taps_far, near, centre)
        )

    norms = over_rows(stats, count, per_group, affine[:, 0], affine[:, 1], make_edge)
    blocks = gathered(packed, norms[0])
    edges = gathered(edge_box[0], norms[0])
    fields = [f for two in zip(blocks, edges) for f in two]
    when, _ = lax.optimization_barrier((src, edge_box[0]))
    taps_two = pl.pallas_call(
        fetch_taps,
        out_shape=jax.ShapeDtypeStruct((n, 3, 3, here, here), BF16),
        in_specs=[SMEM, HBM],
        out_specs=VMEM,
        scratch_shapes=[pltpu.SemaphoreType.DMA((3, n))],
        compiler_params=params(8),
        name="fetch_two",
    )(when, in_hbm(conv_two))
    near = pl.pallas_call(
        lambda *refs: second_near(rows, width, *refs),
        out_shape=jax.ShapeDtypeStruct(parts_shape, F32),
        in_specs=[SMEM] + [VMEM] * 7,
        out_specs=VMEM,
        scratch_shapes=[pltpu.VMEM((2, count + 2 * width, here), BF16)],
        compiler_params=params(12),
        name="two_near",
    )(flags, *fields[:4], *norms[:2], taps_two)
    fields = fields[:4] + list(
        lax.optimization_barrier((near, *fields[4:]))
    )
    near = fields.pop(4)
    y_two, packed, stats = pl.pallas_call(
        lambda *refs: second_far(rows, width, per_group, n - 2, *refs),
        out_shape=(jax.ShapeDtypeStruct(y_shape, F32), packed_shape, stats_shape),
        in_specs=[SMEM] + [VMEM] * (3 * (n - 2) + 2),
        out_specs=(VMEM, VMEM, VMEM),
        scratch_shapes=[
            pltpu.VMEM(parts_shape, F32),
            pltpu.VMEM((n - 2, count + 2 * width, here), BF16),
        ],
        compiler_params=params(12),
        name="two_far",
    )(flags, *fields[4:], *norms[2:], taps_two, near)

    norms = over_rows(stats, count, per_group, affine[:, 2], affine[:, 3])
    blocks = gathered(packed, norms[0])
    when, _ = lax.optimization_barrier((src, packed))
    head_in = pl.pallas_call(
        fetch_head,
        out_shape=jax.ShapeDtypeStruct((n, here, vocab_here), BF16),
        in_specs=[SMEM, HBM],
        out_specs=VMEM,
        scratch_shapes=[pltpu.SemaphoreType.DMA((n,))],
        compiler_params=params(8),
        name="fetch_head",
    )(when, in_hbm(head_weight))
    features = start.astype(F32) + (y_two * norms[0][0, :1] + norms[0][1, :1])
    features = features.astype(BF16).reshape(rows, width, here)

    ids = token_ids.reshape(-1, 1) - lax.axis_index("cols") * vocab_here
    ids = ids - lax.broadcasted_iota(jnp.int32, (1, 128), 1)
    tile = min(512, vocab_here)
    state = pl.pallas_call(
        lambda *refs: head(count, n, tile, *refs),
        out_shape=jax.ShapeDtypeStruct((8, count), F32),
        in_specs=[VMEM] * (3 * n + 2),
        out_specs=VMEM,
        scratch_shapes=[
            pltpu.VMEM((n, count, here), BF16),
            pltpu.VMEM((2, count, tile), F32),
            pltpu.VMEM((count, 128), F32),
            pltpu.VMEM((count, 128), F32),
            pltpu.VMEM((count, 128), F32),
        ],
        compiler_params=params(16),
        name="head",
    )(*mains, *blocks, *norms, head_in, ids)
    step = 1
    while step < n:
        other = lax.ppermute(state, "cols", [(i, i ^ step) for i in range(n)])
        high = jnp.maximum(state[0], other[0])
        total = state[1] * jnp.exp(state[0] - high) + other[1] * jnp.exp(other[0] - high)
        state = jnp.stack([high, total, state[2] + other[2]])
        step *= 2
    logp = (state[2] - state[0] - jnp.log(state[1])).reshape(rows, width)
    slice_width = width // n
    token_logp = lax.dynamic_slice_in_dim(
        logp, lax.axis_index("cols") * slice_width, slice_width, 1
    )
    return (features, token_logp)


def solution(mesh):
    in_specs = (
        P("rows", None),
        P("rows", None),
        P("rows"),
        P(None, "cols"),
        P("cols"),
        P(None, None, None, "cols"),
        P("cols"),
        P("cols"),
        P(None, None, None, "cols"),
        P("cols"),
        P("cols"),
        P(None, "cols"),
    )
    out_specs = (P("rows", None, "cols"), P("rows", "cols"))
    return jax.shard_map(step_of, mesh=mesh, in_specs=in_specs, out_specs=out_specs, check_vma=False)
```

```python
import jax
import jax.numpy as jnp
from jax import lax
from jax.experimental import pallas as pl
from jax.experimental.pallas import tpu as pltpu
from jax.sharding import PartitionSpec as P


GROUPS = 32
EPS = 1e-05
PAD = 16
F32 = jnp.float32
BF16 = jnp.bfloat16
VMEM = pl.BlockSpec(memory_space=pltpu.VMEM)
SMEM = pl.BlockSpec(memory_space=pltpu.SMEM)
HBM = pl.BlockSpec(memory_space=pltpu.HBM)


def swap(value):
    n = lax.axis_size("cols")
    return lax.ppermute(value, "cols", [(i, i ^ 1) for i in range(n)])


def cross(value):
    n = lax.axis_size("cols")
    return [
        lax.ppermute(value, "cols", [(i, (i + 2 * s) % n) for i in range(n)])
        for s in range(1, n // 2)
    ]


def sources():
    n = lax.axis_size("cols")
    me = lax.axis_index("cols")
    out = []
    for s in range(n // 2):
        same = lax.rem(me + n - 2 * s, n)
        out += [same, same ^ 1]
    return out


def gathered(value, after=None):
    out = [value, swap(value)]
    for far in cross(value):
        if after is not None:
            far, _ = lax.optimization_barrier((far, after))
        out += [far, swap(far)]
    return out


def far_blocks(values, after):
    out = []
    for far in values:
        far, _ = lax.optimization_barrier((far, after))
        out += [far, swap(far)]
    return out


def upward(value):
    n = lax.axis_size("rows")
    return lax.ppermute(value, "rows", [(i, i + 1) for i in range(n - 1)])


def downward(value):
    n = lax.axis_size("rows")
    return lax.ppermute(value, "rows", [(i + 1, i) for i in range(n - 1)])


def tile_sum(value):
    return jnp.sum(value, axis=0, keepdims=True)


def load_taps(src, first, w, held, sems):
    here = w.shape[3]
    copies = []
    for b in range(3):
        for k in range(held.shape[0]):
            at = pl.multiple_of(src[first + k] * here, here)
            copy = pltpu.make_async_copy(
                w.at[:, b, pl.ds(at, here), :], held.at[k, b], sems.at[b, k]
            )
            copy.start()
            copies.append(copy)
    return copies


def taps(fields, held, b, i, total):
    for k, field in enumerate(fields):
        for a in range(3):
            part = jnp.dot(field(a + i), held[k, b, a], preferred_element_type=F32)
            total = part if total is None else total + part
    return total


def joined_taps(before, here, after):
    width = here.shape[0]
    col = lax.broadcasted_iota(jnp.int32, here.shape, 0)
    left = jnp.where(col == 0, 0.0, pltpu.roll(before, 1, 0))
    right = jnp.where(col == width - 1, 0.0, pltpu.roll(after, width - 1, 0))
    return here + left + right


def finish(parts, y_ref, packed_ref, stats_ref, rows, width, per_group, out=None):
    here = y_ref.shape[1]
    count = rows * width
    total = jnp.zeros((1, here), F32)
    for i in range(rows):
        y = joined_taps(parts[0, i], parts[1, i], parts[2, i])
        y_ref[i * width : (i + 1) * width, :] = y
        total = total + tile_sum(y)
    if out is not None:
        copy = pltpu.make_async_copy(y_ref, *out)
        copy.start()
    mean = total / count
    centre = mean.astype(BF16).astype(F32)
    square = jnp.zeros((1, here), F32)
    for i in range(rows):
        dev = y_ref[i * width : (i + 1) * width, :] - centre
        packed_ref[i * width : (i + 1) * width, :] = dev.astype(BF16)
        square = square + tile_sum(dev * dev)
    packed_ref[count : count + PAD, :] = jnp.broadcast_to(centre, (PAD, here)).astype(BF16)
    spread = square - count * (mean - centre) * (mean - centre)
    same = (
        lax.broadcasted_iota(jnp.int32, (here, here), 0) // per_group
        == lax.broadcasted_iota(jnp.int32, (here, here), 1) // per_group
    ).astype(F32)

    def over_group(value):
        return jnp.dot(
            jnp.broadcast_to(value, (8, here)),
            same,
            precision=lax.Precision.HIGHEST,
            preferred_element_type=F32,
        )

    mid = over_group(mean) / per_group
    away = mean - mid[:1]
    stats_ref[0] = mid
    stats_ref[1] = over_group(spread + count * away * away)
    if out is not None:
        copy.wait()


def reader(rows, width, main, inner, outer=None):
    def read(r):
        if r == 0:
            return outer[0:width, :]
        if r == 1:
            return inner[0:width, :]
        if r == rows + 2:
            return inner[width : 2 * width, :]
        if r == rows + 3:
            return outer[width : 2 * width, :]
        return main[(r - 2) * width : (r - 1) * width, :]

    return read


def conv_near(rows, width, src, *refs):
    fields, (w, parts, far, held, sems, far_sems) = refs[:6], refs[6:]
    copies = load_taps(src, 0, w, held, sems)
    later = load_taps(src, 2, w, far, far_sems)
    readers = [reader(rows, width, *fields[3 * k : 3 * k + 3]) for k in range(2)]
    for b in range(3):
        for copy in copies[2 * b : 2 * b + 2]:
            copy.wait()
        for i in range(rows + 2):
            parts[b, i] = taps(readers, held, b, i, None)
    for copy in later:
        copy.wait()


def fetch_taps(src, w, held, sems):
    for copy in load_taps(src, 0, w, held, sems):
        copy.wait()


def fetch_head(src, w, held, sems):
    n, here = held.shape[0], held.shape[1]
    copies = []
    for k in range(n):
        at = pl.multiple_of(src[k] * here, here)
        copies.append(pltpu.make_async_copy(w.at[pl.ds(at, here), :], held.at[k], sems.at[k]))
        copies[-1].start()
    for copy in copies:
        copy.wait()


def conv_far(rows, width, per_group, *refs):
    fields, (held, before, packed, stats, parts, y) = refs[:-6], refs[-6:]
    readers = [reader(rows, width, *fields[k : k + 2]) for k in range(0, len(fields), 2)]
    for b in range(3):
        for i in range(rows):
            parts[b, i] = taps(readers, held, b, i + 1, before[b, i + 1])
    finish(parts, y, packed, stats, rows, width, per_group)


def conv_edge(rows, width, *refs):
    fields, (held, before, packed, out) = refs[:-4], refs[-4:]
    readers = [reader(rows, width, *fields[k : k + 3]) for k in range(0, len(fields), 3)]
    count = rows * width
    centre = packed[count : count + PAD, :].astype(F32)[:1]
    for j, i in enumerate((0, rows + 1)):
        y = joined_taps(*[taps(readers, held, b, i, before[b, i]) for b in range(3)])
        out[j * width : (j + 1) * width, :] = (y - centre).astype(BF16)


def activated(rows, width, flags, fields, norms, hidden):
    count = rows * width
    for k in range(len(norms)):
        main, edge = fields[2 * k : 2 * k + 2]
        scale = norms[k][0][:1]
        mid = main[count : count + PAD, :].astype(F32)[:1]
        shift = mid * scale + norms[k][1][:1]
        for r in range(rows + 2):
            if r == 0:
                v = edge[0:width, :]
            elif r == rows + 1:
                v = edge[width : 2 * width, :]
            else:
                v = main[(r - 1) * width : r * width, :]
            v = v.astype(F32) * scale + shift
            v = v * (0.5 + 0.5 * jnp.tanh(0.5 * v))
            if r == 0:
                v = jnp.where(flags[0] > 0, v, 0.0)
            if r == rows + 1:
                v = jnp.where(flags[1] > 0, v, 0.0)
            hidden[k, r * width : (r + 1) * width, :] = v.astype(BF16)
    return [
        (lambda r, k=k: hidden[k, r * width : (r + 1) * width, :]) for k in range(len(norms))
    ]


def second_near(rows, width, flags, *refs):
    fields, norms, (held, parts, hidden) = refs[:4], refs[4:6], refs[6:]
    readers = activated(rows, width, flags, fields, norms, hidden)
    for b in range(3):
        for i in range(rows):
            parts[b, i] = taps(readers, held, b, i, None)


def second_far(rows, width, per_group, n, flags, *refs):
    fields, norms = refs[: 2 * n], refs[2 * n : 3 * n]
    held, near, y, packed, stats, parts, hidden = refs[3 * n :]
    held = held.at[2:]
    readers = activated(rows, width, flags, fields, norms, hidden)
    for b in range(3):
        for i in range(rows):
            parts[b, i] = taps(readers, held, b, i, near[b, i])
    finish(parts, y, packed, stats, rows, width, per_group)


def head(count, n, tile, *refs):
    starts, devs, norms = refs[:n], refs[n : 2 * n], refs[2 * n : 3 * n]
    held, ids, out, feat, logits, top, summed, picked = refs[3 * n :]
    step = 256
    tiles = held.shape[2] // tile
    for k in range(n):
        scale = norms[k][0][:1]
        mid = devs[k][count : count + PAD, :].astype(F32)[:1]
        shift = mid * scale + norms[k][1][:1]
        for r in range(0, count, step):
            value = devs[k][r : r + step, :].astype(F32) * scale + shift
            feat[k, r : r + step, :] = (starts[k][r : r + step, :].astype(F32) + value).astype(BF16)
    top[...] = jnp.full(top.shape, -jnp.inf, F32)
    summed[...] = jnp.zeros(summed.shape, F32)
    picked[...] = jnp.zeros(picked.shape, F32)

    def multiply(t, slot):
        total = None
        for k in range(n):
            part = jnp.dot(
                feat[k],
                held[k, :, pl.ds(pl.multiple_of(t * tile, tile), tile)],
                preferred_element_type=F32,
            )
            total = part if total is None else total + part
        logits[slot] = total

    def reduce(t, slot):
        for r in range(0, count, 64):
            rows = slice(r, r + 64)
            pieces = [logits[slot, rows, g : g + 128] for g in range(0, tile, 128)]
            old = top[rows, :]
            new = old
            for piece in pieces:
                new = jnp.maximum(new, piece)
            total = summed[rows, :] * jnp.exp(old - new)
            hit = picked[rows, :]
            rel = ids[rows, :] - t * tile
            for g, piece in enumerate(pieces):
                total = total + jnp.exp(piece - new)
                hit = jnp.where(rel == g * 128, piece, hit)
            top[rows, :] = new
            summed[rows, :] = total
            picked[rows, :] = hit

    multiply(0, 0)

    def body(t, carry):
        multiply(t, lax.rem(t, 2))
        reduce(t - 1, lax.rem(t + 1, 2))
        return carry

    lax.fori_loop(1, tiles, body, 0)
    reduce(tiles - 1, (tiles - 1) % 2)
    lane = lax.broadcasted_iota(jnp.int32, (128, 128), 1)
    for r in range(0, count, 128):
        rows = slice(r, r + 128)
        high = jnp.max(top[rows, :], axis=1, keepdims=True)
        total = jnp.sum(summed[rows, :] * jnp.exp(top[rows, :] - high), axis=1, keepdims=True)
        hit = jnp.sum(picked[rows, :], axis=1, keepdims=True)
        stacked = jnp.where(lane == 0, high, jnp.where(lane == 1, total, hit))
        out[:, rows] = jnp.transpose(stacked)[:8]


def in_hbm(value):
    return pltpu.with_memory_space_constraint(value, pltpu.HBM)


def params(mib):
    return pltpu.CompilerParams(vmem_limit_bytes=mib << 20)


def over_rows(stats, count, per_group, gains, biases, between=None):
    stats = jnp.stack([stats] + cross(stats))
    population = float(count * per_group)
    n = lax.axis_size("rows")
    step = 1
    while step < n:
        radix = 4 if step > 1 and n // step % 4 == 0 else 2
        others = []
        for j in range(1, radix):
            move = [(i, i ^ (step * j)) for i in range(n)]
            others.append(lax.ppermute(stats, "rows", move))
        states = [stats] + others
        mid = sum(t[:, 0] for t in states) / radix
        away = sum((t[:, 0] - mid) * (t[:, 0] - mid) for t in states)
        stats = jnp.stack([mid, sum(t[:, 1] for t in states) + population * away], axis=1)
        population *= radix
        step *= radix
        if between is not None:
            between(stats)
            between = None
    scale = gains / jnp.sqrt(stats[:, 1] / population + EPS)
    mine = jnp.stack([scale, biases - stats[:, 0] * scale], axis=1)
    other = swap(mine)
    return [f for k in range(mine.shape[0]) for f in (mine[k], other[k])]


def step_of(
    token_ids,
    keep_mask,
    remask_order,
    embed_table,
    mask_embed,
    conv_one,
    gain_one,
    bias_one,
    conv_two,
    gain_two,
    bias_two,
    head_weight,
):
    rows, width = token_ids.shape
    n_rows = lax.axis_size("rows")
    n = lax.axis_size("cols")
    height = rows * n_rows
    here = gain_one.shape[0]
    per_group = here * n // GROUPS
    count = rows * width
    me_row = lax.axis_index("rows")
    flags = jnp.stack([me_row > 0, me_row < n_rows - 1]).astype(jnp.int32)
    src = jnp.stack(sources()).astype(jnp.int32)

    def look(codes):
        rows_of = jnp.take(embed_table, jnp.maximum(codes - 2, 0), axis=0, mode="clip")
        rows_of = jnp.where(codes[:, None] == 1, mask_embed[None, :], rows_of)
        return jnp.where(codes[:, None] == 0, 0, rows_of)

    looked = jnp.take(embed_table, token_ids.reshape(-1), axis=0, mode="clip")
    main_far = cross(looked)
    token_ids, keep_mask, remask_order, looked = lax.optimization_barrier(
        (token_ids, keep_mask, remask_order, looked)
    )
    visible = (keep_mask.reshape(-1) == 1) | (remask_order >= height * width // 2)
    code = jnp.where(visible, token_ids.reshape(-1) + 2, 1)
    start = jnp.where(visible[:, None], looked, mask_embed[None, :])
    above, below = upward(code[count - 2 * width :]), downward(code[: 2 * width])
    halo = look(
        jnp.concatenate([above[width:], below[:width], above[:width], below[width:]])
    )
    inner, outer = halo[: 2 * width], halo[2 * width :]
    mains = [start, swap(start)]
    inners, inner_far = [inner, swap(inner)], cross(inner)
    outers, outer_far = [outer, swap(outer)], cross(outer)

    packed_shape = jax.ShapeDtypeStruct((count + PAD, here), BF16)
    stats_shape = jax.ShapeDtypeStruct((2, 8, here), F32)
    parts_shape = (3, rows, width, here)
    y_shape = (count, here)
    own = jnp.stack([gain_one, bias_one, gain_two, bias_two, mask_embed.astype(F32)])
    own = jnp.broadcast_to(own[:, None], (5, 8, here))
    affine = jnp.stack([own] + cross(own))
    mask_far = affine[1:, 4, 0].astype(BF16)
    main_far = [
        jnp.where(visible[:, None], far, mask_far[k]) for k, far in enumerate(main_far)
    ]
    fields = [f for k in range(2) for f in (mains[k], inners[k], outers[k])]
    vocab_here = head_weight.shape[1]
    near, taps_far = pl.pallas_call(
        lambda *refs: conv_near(rows, width, *refs),
        out_shape=(
            jax.ShapeDtypeStruct((3, rows + 2, width, here), F32),
            jax.ShapeDtypeStruct((n - 2, 3, 3, here, here), BF16),
        ),
        in_specs=[SMEM] + [VMEM] * 6 + [HBM],
        out_specs=(VMEM,) * 2,
        scratch_shapes=[
            pltpu.VMEM((2, 3, 3, here, here), BF16),
            pltpu.SemaphoreType.DMA((3, 2)),
            pltpu.SemaphoreType.DMA((3, n - 2)),
        ],
        compiler_params=params(12),
        name="conv_near",
    )(src, *fields, in_hbm(conv_one))
    mains += far_blocks(main_far, near)
    inners += far_blocks(inner_far, near)
    outers += far_blocks(outer_far, near)
    fields = [f for k in range(2, n) for f in (mains[k], inners[k])]
    packed, stats = pl.pallas_call(
        lambda *refs: conv_far(rows, width, per_group, *refs),
        out_shape=(packed_shape, stats_shape),
        in_specs=[VMEM] * (len(fields) + 2),
        out_specs=(VMEM, VMEM),
        scratch_shapes=[pltpu.VMEM(parts_shape, F32), pltpu.VMEM(y_shape, F32)],
        compiler_params=params(12),
        name="conv_far",
    )(*fields, taps_far, near)
    fields = [f for k in range(2, n) for f in (mains[k], inners[k], outers[k])]
    edge_box = []

    def make_edge(state):
        centre, _ = lax.optimization_barrier((packed, state))
        edge_box.append(
            pl.pallas_call(
                lambda *refs: conv_edge(rows, width, *refs),
                out_shape=jax.ShapeDtypeStruct((2 * width, here), BF16),
                in_specs=[VMEM] * (len(fields) + 3),
                out_specs=VMEM,
                compiler_params=params(8),
                name="conv_edge",
            )(*fields, taps_far, near, centre)
        )

    norms = over_rows(stats, count, per_group, affine[:, 0], affine[:, 1], make_edge)
    blocks = gathered(packed, norms[0])
    edges = gathered(edge_box[0], norms[0])
    fields = [f for two in zip(blocks, edges) for f in two]
    when, _ = lax.optimization_barrier((src, edge_box[0]))
    taps_two = pl.pallas_call(
        fetch_taps,
        out_shape=jax.ShapeDtypeStruct((n, 3, 3, here, here), BF16),
        in_specs=[SMEM, HBM],
        out_specs=VMEM,
        scratch_shapes=[pltpu.SemaphoreType.DMA((3, n))],
        compiler_params=params(8),
        name="fetch_two",
    )(when, in_hbm(conv_two))
    near = pl.pallas_call(
        lambda *refs: second_near(rows, width, *refs),
        out_shape=jax.ShapeDtypeStruct(parts_shape, F32),
        in_specs=[SMEM] + [VMEM] * 7,
        out_specs=VMEM,
        scratch_shapes=[pltpu.VMEM((2, count + 2 * width, here), BF16)],
        compiler_params=params(12),
        name="two_near",
    )(flags, *fields[:4], *norms[:2], taps_two)
    fields = fields[:4] + list(
        lax.optimization_barrier((near, *fields[4:]))
    )
    near = fields.pop(4)
    y_two, packed, stats = pl.pallas_call(
        lambda *refs: second_far(rows, width, per_group, n - 2, *refs),
        out_shape=(jax.ShapeDtypeStruct(y_shape, F32), packed_shape, stats_shape),
        in_specs=[SMEM] + [VMEM] * (3 * (n - 2) + 2),
        out_specs=(VMEM, VMEM, VMEM),
        scratch_shapes=[
            pltpu.VMEM(parts_shape, F32),
            pltpu.VMEM((n - 2, count + 2 * width, here), BF16),
        ],
        compiler_params=params(12),
        name="two_far",
    )(flags, *fields[4:], *norms[2:], taps_two, near)

    norms = over_rows(stats, count, per_group, affine[:, 2], affine[:, 3])
    blocks = gathered(packed, norms[0])
    when, _ = lax.optimization_barrier((src, packed))
    head_in = pl.pallas_call(
        fetch_head,
        out_shape=jax.ShapeDtypeStruct((n, here, vocab_here), BF16),
        in_specs=[SMEM, HBM],
        out_specs=VMEM,
        scratch_shapes=[pltpu.SemaphoreType.DMA((n,))],
        compiler_params=params(8),
        name="fetch_head",
    )(when, in_hbm(head_weight))
    features = start.astype(F32) + (y_two * norms[0][0, :1] + norms[0][1, :1])
    features = features.astype(BF16).reshape(rows, width, here)

    ids = token_ids.reshape(-1, 1) - lax.axis_index("cols") * vocab_here
    ids = ids - lax.broadcasted_iota(jnp.int32, (1, 128), 1)
    ids, features = lax.optimization_barrier((ids, features))
    tile = min(512, vocab_here)
    state = pl.pallas_call(
        lambda *refs: head(count, n, tile, *refs),
        out_shape=jax.ShapeDtypeStruct((8, count), F32),
        in_specs=[VMEM] * (3 * n + 2),
        out_specs=VMEM,
        scratch_shapes=[
            pltpu.VMEM((n, count, here), BF16),
            pltpu.VMEM((2, count, tile), F32),
            pltpu.VMEM((count, 128), F32),
            pltpu.VMEM((count, 128), F32),
            pltpu.VMEM((count, 128), F32),
        ],
        compiler_params=params(16),
        name="head",
    )(*mains, *blocks, *norms, head_in, ids)
    step = 1
    while step < n:
        other = lax.ppermute(state, "cols", [(i, i ^ step) for i in range(n)])
        high = jnp.maximum(state[0], other[0])
        total = state[1] * jnp.exp(state[0] - high) + other[1] * jnp.exp(other[0] - high)
        state = jnp.stack([high, total, state[2] + other[2]])
        step *= 2
    logp = (state[2] - state[0] - jnp.log(state[1])).reshape(rows, width)
    slice_width = width // n
    token_logp = lax.dynamic_slice_in_dim(
        logp, lax.axis_index("cols") * slice_width, slice_width, 1
    )
    return (features, token_logp)


def solution(mesh):
    in_specs = (
        P("rows", None),
        P("rows", None),
        P("rows"),
        P(None, "cols"),
        P("cols"),
        P(None, None, None, "cols"),
        P("cols"),
        P("cols"),
        P(None, None, None, "cols"),
        P("cols"),
        P("cols"),
        P(None, "cols"),
    )
    out_specs = (P("rows", None, "cols"), P("rows", "cols"))
    return jax.shard_map(step_of, mesh=mesh, in_specs=in_specs, out_specs=out_specs, check_vma=False)
```

```python
import jax
import jax.numpy as jnp
from jax import lax
from jax.experimental import pallas as pl
from jax.experimental.pallas import tpu as pltpu
from jax.sharding import PartitionSpec as P


GROUPS = 32
EPS = 1e-05
PAD = 16
F32 = jnp.float32
BF16 = jnp.bfloat16
VMEM = pl.BlockSpec(memory_space=pltpu.VMEM)
SMEM = pl.BlockSpec(memory_space=pltpu.SMEM)
HBM = pl.BlockSpec(memory_space=pltpu.HBM)


def swap(value):
    n = lax.axis_size("cols")
    return lax.ppermute(value, "cols", [(i, i ^ 1) for i in range(n)])


def cross(value):
    n = lax.axis_size("cols")
    return [
        lax.ppermute(value, "cols", [(i, (i + 2 * s) % n) for i in range(n)])
        for s in range(1, n // 2)
    ]


def sources():
    n = lax.axis_size("cols")
    me = lax.axis_index("cols")
    out = []
    for s in range(n // 2):
        same = lax.rem(me + n - 2 * s, n)
        out += [same, same ^ 1]
    return out


def gathered(value, after=None):
    out = [value, swap(value)]
    for far in cross(value):
        if after is not None:
            far, _ = lax.optimization_barrier((far, after))
        out += [far, swap(far)]
    return out


def far_blocks(values, after):
    out = []
    for far in values:
        far, _ = lax.optimization_barrier((far, after))
        out += [far, swap(far)]
    return out


def upward(value):
    n = lax.axis_size("rows")
    return lax.ppermute(value, "rows", [(i, i + 1) for i in range(n - 1)])


def downward(value):
    n = lax.axis_size("rows")
    return lax.ppermute(value, "rows", [(i + 1, i) for i in range(n - 1)])


def tile_sum(value):
    return jnp.sum(value, axis=0, keepdims=True)


def load_taps(src, first, w, held, sems):
    here = w.shape[3]
    copies = []
    for b in range(3):
        for k in range(held.shape[0]):
            at = pl.multiple_of(src[first + k] * here, here)
            copy = pltpu.make_async_copy(
                w.at[:, b, pl.ds(at, here), :], held.at[k, b], sems.at[b, k]
            )
            copy.start()
            copies.append(copy)
    return copies


def taps(fields, held, b, i, total):
    for k, field in enumerate(fields):
        for a in range(3):
            part = jnp.dot(field(a + i), held[k, b, a], preferred_element_type=F32)
            total = part if total is None else total + part
    return total


def joined_taps(before, here, after):
    width = here.shape[0]
    col = lax.broadcasted_iota(jnp.int32, here.shape, 0)
    left = jnp.where(col == 0, 0.0, pltpu.roll(before, 1, 0))
    right = jnp.where(col == width - 1, 0.0, pltpu.roll(after, width - 1, 0))
    return here + left + right


def finish(parts, y_ref, packed_ref, stats_ref, rows, width, per_group, out=None):
    here = y_ref.shape[1]
    count = rows * width
    total = jnp.zeros((1, here), F32)
    for i in range(rows):
        y = joined_taps(parts[0, i], parts[1, i], parts[2, i])
        y_ref[i * width : (i + 1) * width, :] = y
        total = total + tile_sum(y)
    if out is not None:
        copy = pltpu.make_async_copy(y_ref, *out)
        copy.start()
    mean = total / count
    centre = mean.astype(BF16).astype(F32)
    square = jnp.zeros((1, here), F32)
    for i in range(rows):
        dev = y_ref[i * width : (i + 1) * width, :] - centre
        packed_ref[i * width : (i + 1) * width, :] = dev.astype(BF16)
        square = square + tile_sum(dev * dev)
    packed_ref[count : count + PAD, :] = jnp.broadcast_to(centre, (PAD, here)).astype(BF16)
    spread = square - count * (mean - centre) * (mean - centre)
    same = (
        lax.broadcasted_iota(jnp.int32, (here, here), 0) // per_group
        == lax.broadcasted_iota(jnp.int32, (here, here), 1) // per_group
    ).astype(F32)

    def over_group(value):
        return jnp.dot(
            jnp.broadcast_to(value, (8, here)),
            same,
            precision=lax.Precision.HIGHEST,
            preferred_element_type=F32,
        )

    mid = over_group(mean) / per_group
    away = mean - mid[:1]
    stats_ref[0] = mid
    stats_ref[1] = over_group(spread + count * away * away)
    if out is not None:
        copy.wait()


def reader(rows, width, main, inner, outer=None):
    def read(r):
        if r == 0:
            return outer[0:width, :]
        if r == 1:
            return inner[0:width, :]
        if r == rows + 2:
            return inner[width : 2 * width, :]
        if r == rows + 3:
            return outer[width : 2 * width, :]
        return main[(r - 2) * width : (r - 1) * width, :]

    return read


def conv_near(rows, width, src, *refs):
    fields, (w, parts, far, held, sems, far_sems) = refs[:6], refs[6:]
    copies = load_taps(src, 0, w, held, sems)
    later = load_taps(src, 2, w, far, far_sems)
    readers = [reader(rows, width, *fields[3 * k : 3 * k + 3]) for k in range(2)]
    for b in range(3):
        for copy in copies[2 * b : 2 * b + 2]:
            copy.wait()
        for i in range(rows + 2):
            parts[b, i] = taps(readers, held, b, i, None)
    for copy in later:
        copy.wait()


def fetch_taps(src, w, held, sems):
    for copy in load_taps(src, 0, w, held, sems):
        copy.wait()


def fetch_head(src, w, held, sems):
    n, here = held.shape[0], held.shape[1]
    copies = []
    for k in range(n):
        at = pl.multiple_of(src[k] * here, here)
        copies.append(pltpu.make_async_copy(w.at[pl.ds(at, here), :], held.at[k], sems.at[k]))
        copies[-1].start()
    for copy in copies:
        copy.wait()


def conv_far(rows, width, per_group, *refs):
    fields, (held, before, packed, stats, parts, y) = refs[:-6], refs[-6:]
    readers = [reader(rows, width, *fields[k : k + 2]) for k in range(0, len(fields), 2)]
    for b in range(3):
        for i in range(rows):
            parts[b, i] = taps(readers, held, b, i + 1, before[b, i + 1])
    finish(parts, y, packed, stats, rows, width, per_group)


def conv_edge(rows, width, *refs):
    fields, (held, before, packed, out) = refs[:-4], refs[-4:]
    readers = [reader(rows, width, *fields[k : k + 3]) for k in range(0, len(fields), 3)]
    count = rows * width
    centre = packed[count : count + PAD, :].astype(F32)[:1]
    for j, i in enumerate((0, rows + 1)):
        y = joined_taps(*[taps(readers, held, b, i, before[b, i]) for b in range(3)])
        out[j * width : (j + 1) * width, :] = (y - centre).astype(BF16)


def activated(rows, width, flags, fields, norms, hidden):
    count = rows * width
    for k in range(len(norms)):
        main, edge = fields[2 * k : 2 * k + 2]
        scale = norms[k][0][:1]
        mid = main[count : count + PAD, :].astype(F32)[:1]
        shift = mid * scale + norms[k][1][:1]
        for r in range(rows + 2):
            if r == 0:
                v = edge[0:width, :]
            elif r == rows + 1:
                v = edge[width : 2 * width, :]
            else:
                v = main[(r - 1) * width : r * width, :]
            v = v.astype(F32) * scale + shift
            v = v * (0.5 + 0.5 * jnp.tanh(0.5 * v))
            if r == 0:
                v = jnp.where(flags[0] > 0, v, 0.0)
            if r == rows + 1:
                v = jnp.where(flags[1] > 0, v, 0.0)
            hidden[k, r * width : (r + 1) * width, :] = v.astype(BF16)
    return [
        (lambda r, k=k: hidden[k, r * width : (r + 1) * width, :]) for k in range(len(norms))
    ]


def second_near(rows, width, flags, *refs):
    fields, norms, (held, parts, hidden) = refs[:4], refs[4:6], refs[6:]
    readers = activated(rows, width, flags, fields, norms, hidden)
    for b in range(3):
        for i in range(rows):
            parts[b, i] = taps(readers, held, b, i, None)


def second_far(rows, width, per_group, n, flags, *refs):
    fields, norms = refs[: 2 * n], refs[2 * n : 3 * n]
    held, near, y, packed, stats, parts, hidden = refs[3 * n :]
    held = held.at[2:]
    readers = activated(rows, width, flags, fields, norms, hidden)
    for b in range(3):
        for i in range(rows):
            parts[b, i] = taps(readers, held, b, i, near[b, i])
    finish(parts, y, packed, stats, rows, width, per_group)


def head(count, n, tile, *refs):
    starts, devs, norms = refs[:n], refs[n : 2 * n], refs[2 * n : 3 * n]
    held, ids, out, feat, logits, top, summed, picked = refs[3 * n :]
    step = 256
    tiles = held.shape[2] // tile
    for k in range(n):
        scale = norms[k][0][:1]
        mid = devs[k][count : count + PAD, :].astype(F32)[:1]
        shift = mid * scale + norms[k][1][:1]
        for r in range(0, count, step):
            value = devs[k][r : r + step, :].astype(F32) * scale + shift
            feat[k, r : r + step, :] = (starts[k][r : r + step, :].astype(F32) + value).astype(BF16)
    top[...] = jnp.full(top.shape, -jnp.inf, F32)
    summed[...] = jnp.zeros(summed.shape, F32)
    picked[...] = jnp.zeros(picked.shape, F32)

    def multiply(t, slot):
        total = None
        for k in range(n):
            part = jnp.dot(
                feat[k],
                held[k, :, t * tile : (t + 1) * tile],
                preferred_element_type=F32,
            )
            total = part if total is None else total + part
        logits[slot] = total

    def reduce(t, slot):
        for r in range(0, count, 64):
            rows = slice(r, r + 64)
            pieces = [logits[slot, rows, g : g + 128] for g in range(0, tile, 128)]
            old = top[rows, :]
            new = old
            for piece in pieces:
                new = jnp.maximum(new, piece)
            total = summed[rows, :] * jnp.exp(old - new)
            hit = picked[rows, :]
            rel = ids[rows, :] - t * tile
            for g, piece in enumerate(pieces):
                total = total + jnp.exp(piece - new)
                hit = jnp.where(rel == g * 128, piece, hit)
            top[rows, :] = new
            summed[rows, :] = total
            picked[rows, :] = hit

    for t in range(tiles):
        multiply(t, t % 2)
        reduce(t, t % 2)
    lane = lax.broadcasted_iota(jnp.int32, (128, 128), 1)
    for r in range(0, count, 128):
        rows = slice(r, r + 128)
        high = jnp.max(top[rows, :], axis=1, keepdims=True)
        total = jnp.sum(summed[rows, :] * jnp.exp(top[rows, :] - high), axis=1, keepdims=True)
        hit = jnp.sum(picked[rows, :], axis=1, keepdims=True)
        stacked = jnp.where(lane == 0, high, jnp.where(lane == 1, total, hit))
        out[:, rows] = jnp.transpose(stacked)[:8]


def in_hbm(value):
    return pltpu.with_memory_space_constraint(value, pltpu.HBM)


def params(mib):
    return pltpu.CompilerParams(vmem_limit_bytes=mib << 20)


def over_rows(stats, count, per_group, gains, biases, between=None):
    stats = jnp.stack([stats] + cross(stats))
    population = float(count * per_group)
    n = lax.axis_size("rows")
    step = 1
    while step < n:
        radix = 4 if step > 1 and n // step % 4 == 0 else 2
        others = []
        for j in range(1, radix):
            move = [(i, i ^ (step * j)) for i in range(n)]
            others.append(lax.ppermute(stats, "rows", move))
        states = [stats] + others
        mid = sum(t[:, 0] for t in states) / radix
        away = sum((t[:, 0] - mid) * (t[:, 0] - mid) for t in states)
        stats = jnp.stack([mid, sum(t[:, 1] for t in states) + population * away], axis=1)
        population *= radix
        step *= radix
        if between is not None:
            between(stats)
            between = None
    scale = gains / jnp.sqrt(stats[:, 1] / population + EPS)
    mine = jnp.stack([scale, biases - stats[:, 0] * scale], axis=1)
    other = swap(mine)
    return [f for k in range(mine.shape[0]) for f in (mine[k], other[k])]


def step_of(
    token_ids,
    keep_mask,
    remask_order,
    embed_table,
    mask_embed,
    conv_one,
    gain_one,
    bias_one,
    conv_two,
    gain_two,
    bias_two,
    head_weight,
):
    rows, width = token_ids.shape
    n_rows = lax.axis_size("rows")
    n = lax.axis_size("cols")
    height = rows * n_rows
    here = gain_one.shape[0]
    per_group = here * n // GROUPS
    count = rows * width
    me_row = lax.axis_index("rows")
    flags = jnp.stack([me_row > 0, me_row < n_rows - 1]).astype(jnp.int32)
    src = jnp.stack(sources()).astype(jnp.int32)

    def look(codes):
        rows_of = jnp.take(embed_table, jnp.maximum(codes - 2, 0), axis=0, mode="clip")
        rows_of = jnp.where(codes[:, None] == 1, mask_embed[None, :], rows_of)
        return jnp.where(codes[:, None] == 0, 0, rows_of)

    looked = jnp.take(embed_table, token_ids.reshape(-1), axis=0, mode="clip")
    main_far = cross(looked)
    token_ids, keep_mask, remask_order, looked = lax.optimization_barrier(
        (token_ids, keep_mask, remask_order, looked)
    )
    visible = (keep_mask.reshape(-1) == 1) | (remask_order >= height * width // 2)
    code = jnp.where(visible, token_ids.reshape(-1) + 2, 1)
    start = jnp.where(visible[:, None], looked, mask_embed[None, :])
    above, below = upward(code[count - 2 * width :]), downward(code[: 2 * width])
    halo = look(
        jnp.concatenate([above[width:], below[:width], above[:width], below[width:]])
    )
    inner, outer = halo[: 2 * width], halo[2 * width :]
    mains = [start, swap(start)]
    inners, inner_far = [inner, swap(inner)], cross(inner)
    outers, outer_far = [outer, swap(outer)], cross(outer)

    packed_shape = jax.ShapeDtypeStruct((count + PAD, here), BF16)
    stats_shape = jax.ShapeDtypeStruct((2, 8, here), F32)
    parts_shape = (3, rows, width, here)
    y_shape = (count, here)
    own = jnp.stack([gain_one, bias_one, gain_two, bias_two, mask_embed.astype(F32)])
    own = jnp.broadcast_to(own[:, None], (5, 8, here))
    affine = jnp.stack([own] + cross(own))
    mask_far = affine[1:, 4, 0].astype(BF16)
    main_far = [
        jnp.where(visible[:, None], far, mask_far[k]) for k, far in enumerate(main_far)
    ]
    fields = [f for k in range(2) for f in (mains[k], inners[k], outers[k])]
    vocab_here = head_weight.shape[1]
    near, taps_far = pl.pallas_call(
        lambda *refs: conv_near(rows, width, *refs),
        out_shape=(
            jax.ShapeDtypeStruct((3, rows + 2, width, here), F32),
            jax.ShapeDtypeStruct((n - 2, 3, 3, here, here), BF16),
        ),
        in_specs=[SMEM] + [VMEM] * 6 + [HBM],
        out_specs=(VMEM,) * 2,
        scratch_shapes=[
            pltpu.VMEM((2, 3, 3, here, here), BF16),
            pltpu.SemaphoreType.DMA((3, 2)),
            pltpu.SemaphoreType.DMA((3, n - 2)),
        ],
        compiler_params=params(12),
        name="conv_near",
    )(src, *fields, in_hbm(conv_one))
    mains += far_blocks(main_far, near)
    inners += far_blocks(inner_far, near)
    outers += far_blocks(outer_far, near)
    fields = [f for k in range(2, n) for f in (mains[k], inners[k])]
    packed, stats = pl.pallas_call(
        lambda *refs: conv_far(rows, width, per_group, *refs),
        out_shape=(packed_shape, stats_shape),
        in_specs=[VMEM] * (len(fields) + 2),
        out_specs=(VMEM, VMEM),
        scratch_shapes=[pltpu.VMEM(parts_shape, F32), pltpu.VMEM(y_shape, F32)],
        compiler_params=params(12),
        name="conv_far",
    )(*fields, taps_far, near)
    fields = [f for k in range(2, n) for f in (mains[k], inners[k], outers[k])]
    edge_box = []

    def make_edge(state):
        centre, _ = lax.optimization_barrier((packed, state))
        edge_box.append(
            pl.pallas_call(
                lambda *refs: conv_edge(rows, width, *refs),
                out_shape=jax.ShapeDtypeStruct((2 * width, here), BF16),
                in_specs=[VMEM] * (len(fields) + 3),
                out_specs=VMEM,
                compiler_params=params(8),
                name="conv_edge",
            )(*fields, taps_far, near, centre)
        )

    norms = over_rows(stats, count, per_group, affine[:, 0], affine[:, 1], make_edge)
    blocks = gathered(packed, norms[0])
    edges = gathered(edge_box[0], norms[0])
    fields = [f for two in zip(blocks, edges) for f in two]
    when, _ = lax.optimization_barrier((src, edge_box[0]))
    taps_two = pl.pallas_call(
        fetch_taps,
        out_shape=jax.ShapeDtypeStruct((n, 3, 3, here, here), BF16),
        in_specs=[SMEM, HBM],
        out_specs=VMEM,
        scratch_shapes=[pltpu.SemaphoreType.DMA((3, n))],
        compiler_params=params(8),
        name="fetch_two",
    )(when, in_hbm(conv_two))
    near = pl.pallas_call(
        lambda *refs: second_near(rows, width, *refs),
        out_shape=jax.ShapeDtypeStruct(parts_shape, F32),
        in_specs=[SMEM] + [VMEM] * 7,
        out_specs=VMEM,
        scratch_shapes=[pltpu.VMEM((2, count + 2 * width, here), BF16)],
        compiler_params=params(12),
        name="two_near",
    )(flags, *fields[:4], *norms[:2], taps_two)
    fields = fields[:4] + list(
        lax.optimization_barrier((near, *fields[4:]))
    )
    near = fields.pop(4)
    y_two, packed, stats = pl.pallas_call(
        lambda *refs: second_far(rows, width, per_group, n - 2, *refs),
        out_shape=(jax.ShapeDtypeStruct(y_shape, F32), packed_shape, stats_shape),
        in_specs=[SMEM] + [VMEM] * (3 * (n - 2) + 2),
        out_specs=(VMEM, VMEM, VMEM),
        scratch_shapes=[
            pltpu.VMEM(parts_shape, F32),
            pltpu.VMEM((n - 2, count + 2 * width, here), BF16),
        ],
        compiler_params=params(12),
        name="two_far",
    )(flags, *fields[4:], *norms[2:], taps_two, near)

    norms = over_rows(stats, count, per_group, affine[:, 2], affine[:, 3])
    blocks = gathered(packed, norms[0])
    when, _ = lax.optimization_barrier((src, packed))
    head_in = pl.pallas_call(
        fetch_head,
        out_shape=jax.ShapeDtypeStruct((n, here, vocab_here), BF16),
        in_specs=[SMEM, HBM],
        out_specs=VMEM,
        scratch_shapes=[pltpu.SemaphoreType.DMA((n,))],
        compiler_params=params(8),
        name="fetch_head",
    )(when, in_hbm(head_weight))
    features = start.astype(F32) + (y_two * norms[0][0, :1] + norms[0][1, :1])
    features = features.astype(BF16).reshape(rows, width, here)

    ids = token_ids.reshape(-1, 1) - lax.axis_index("cols") * vocab_here
    ids = ids - lax.broadcasted_iota(jnp.int32, (1, 128), 1)
    ids, features = lax.optimization_barrier((ids, features))
    tile = min(512, vocab_here)
    state = pl.pallas_call(
        lambda *refs: head(count, n, tile, *refs),
        out_shape=jax.ShapeDtypeStruct((8, count), F32),
        in_specs=[VMEM] * (3 * n + 2),
        out_specs=VMEM,
        scratch_shapes=[
            pltpu.VMEM((n, count, here), BF16),
            pltpu.VMEM((2, count, tile), F32),
            pltpu.VMEM((count, 128), F32),
            pltpu.VMEM((count, 128), F32),
            pltpu.VMEM((count, 128), F32),
        ],
        compiler_params=params(16),
        name="head",
    )(*mains, *blocks, *norms, head_in, ids)
    step = 1
    while step < n:
        other = lax.ppermute(state, "cols", [(i, i ^ step) for i in range(n)])
        high = jnp.maximum(state[0], other[0])
        total = state[1] * jnp.exp(state[0] - high) + other[1] * jnp.exp(other[0] - high)
        state = jnp.stack([high, total, state[2] + other[2]])
        step *= 2
    logp = (state[2] - state[0] - jnp.log(state[1])).reshape(rows, width)
    slice_width = width // n
    token_logp = lax.dynamic_slice_in_dim(
        logp, lax.axis_index("cols") * slice_width, slice_width, 1
    )
    return (features, token_logp)


def solution(mesh):
    in_specs = (
        P("rows", None),
        P("rows", None),
        P("rows"),
        P(None, "cols"),
        P("cols"),
        P(None, None, None, "cols"),
        P("cols"),
        P("cols"),
        P(None, None, None, "cols"),
        P("cols"),
        P("cols"),
        P(None, "cols"),
    )
    out_specs = (P("rows", None, "cols"), P("rows", "cols"))
    return jax.shard_map(step_of, mesh=mesh, in_specs=in_specs, out_specs=out_specs, check_vma=False)
```

```python
import jax
import jax.numpy as jnp
from jax import lax
from jax.experimental import pallas as pl
from jax.experimental.pallas import tpu as pltpu
from jax.sharding import PartitionSpec as P


GROUPS = 32
EPS = 1e-05
PAD = 16
F32 = jnp.float32
BF16 = jnp.bfloat16
VMEM = pl.BlockSpec(memory_space=pltpu.VMEM)
SMEM = pl.BlockSpec(memory_space=pltpu.SMEM)
HBM = pl.BlockSpec(memory_space=pltpu.HBM)


def swap(value):
    n = lax.axis_size("cols")
    return lax.ppermute(value, "cols", [(i, i ^ 1) for i in range(n)])


def cross(value):
    n = lax.axis_size("cols")
    return [
        lax.ppermute(value, "cols", [(i, (i + 2 * s) % n) for i in range(n)])
        for s in range(1, n // 2)
    ]


def sources():
    n = lax.axis_size("cols")
    me = lax.axis_index("cols")
    out = []
    for s in range(n // 2):
        same = lax.rem(me + n - 2 * s, n)
        out += [same, same ^ 1]
    return out


def gathered(value, after=None):
    out = [value, swap(value)]
    for far in cross(value):
        if after is not None:
            far, _ = lax.optimization_barrier((far, after))
        out += [far, swap(far)]
    return out


def far_blocks(values, after):
    out = []
    for far in values:
        far, _ = lax.optimization_barrier((far, after))
        out += [far, swap(far)]
    return out


def upward(value):
    n = lax.axis_size("rows")
    return lax.ppermute(value, "rows", [(i, i + 1) for i in range(n - 1)])


def downward(value):
    n = lax.axis_size("rows")
    return lax.ppermute(value, "rows", [(i + 1, i) for i in range(n - 1)])


def tile_sum(value):
    return jnp.sum(value, axis=0, keepdims=True)


def load_taps(src, first, w, held, sems):
    here = w.shape[3]
    copies = []
    for b in range(3):
        for k in range(held.shape[0]):
            at = pl.multiple_of(src[first + k] * here, here)
            copy = pltpu.make_async_copy(
                w.at[:, b, pl.ds(at, here), :], held.at[k, b], sems.at[b, k]
            )
            copy.start()
            copies.append(copy)
    return copies


def taps(fields, held, b, i, total):
    for k, field in enumerate(fields):
        for a in range(3):
            part = jnp.dot(field(a + i), held[k, b, a], preferred_element_type=F32)
            total = part if total is None else total + part
    return total


def joined_taps(before, here, after):
    width = here.shape[0]
    col = lax.broadcasted_iota(jnp.int32, here.shape, 0)
    left = jnp.where(col == 0, 0.0, pltpu.roll(before, 1, 0))
    right = jnp.where(col == width - 1, 0.0, pltpu.roll(after, width - 1, 0))
    return here + left + right


def finish(parts, y_ref, packed_ref, stats_ref, rows, width, per_group, out=None):
    here = y_ref.shape[1]
    count = rows * width
    total = jnp.zeros((1, here), F32)
    for i in range(rows):
        y = joined_taps(parts[0, i], parts[1, i], parts[2, i])
        y_ref[i * width : (i + 1) * width, :] = y
        total = total + tile_sum(y)
    if out is not None:
        copy = pltpu.make_async_copy(y_ref, *out)
        copy.start()
    mean = total / count
    centre = mean.astype(BF16).astype(F32)
    square = jnp.zeros((1, here), F32)
    for i in range(rows):
        dev = y_ref[i * width : (i + 1) * width, :] - centre
        packed_ref[i * width : (i + 1) * width, :] = dev.astype(BF16)
        square = square + tile_sum(dev * dev)
    packed_ref[count : count + PAD, :] = jnp.broadcast_to(centre, (PAD, here)).astype(BF16)
    spread = square - count * (mean - centre) * (mean - centre)
    same = (
        lax.broadcasted_iota(jnp.int32, (here, here), 0) // per_group
        == lax.broadcasted_iota(jnp.int32, (here, here), 1) // per_group
    ).astype(F32)

    def over_group(value):
        return jnp.dot(
            jnp.broadcast_to(value, (8, here)),
            same,
            precision=lax.Precision.HIGHEST,
            preferred_element_type=F32,
        )

    mid = over_group(mean) / per_group
    away = mean - mid[:1]
    stats_ref[0] = mid
    stats_ref[1] = over_group(spread + count * away * away)
    if out is not None:
        copy.wait()


def reader(rows, width, main, inner, outer=None):
    def read(r):
        if r == 0:
            return outer[0:width, :]
        if r == 1:
            return inner[0:width, :]
        if r == rows + 2:
            return inner[width : 2 * width, :]
        if r == rows + 3:
            return outer[width : 2 * width, :]
        return main[(r - 2) * width : (r - 1) * width, :]

    return read


def conv_near(rows, width, src, *refs):
    fields, (w, parts, far, held, sems, far_sems) = refs[:6], refs[6:]
    copies = load_taps(src, 0, w, held, sems)
    later = load_taps(src, 2, w, far, far_sems)
    readers = [reader(rows, width, *fields[3 * k : 3 * k + 3]) for k in range(2)]
    for b in range(3):
        for copy in copies[2 * b : 2 * b + 2]:
            copy.wait()
        for i in range(rows + 2):
            parts[b, i] = taps(readers, held, b, i, None)
    for copy in later:
        copy.wait()


def fetch_taps(src, w, held, sems):
    for copy in load_taps(src, 0, w, held, sems):
        copy.wait()


def fetch_head(src, w, held, sems):
    n, here = held.shape[0], held.shape[1]
    copies = []
    for k in range(n):
        at = pl.multiple_of(src[k] * here, here)
        copies.append(pltpu.make_async_copy(w.at[pl.ds(at, here), :], held.at[k], sems.at[k]))
        copies[-1].start()
    for copy in copies:
        copy.wait()


def conv_far(rows, width, per_group, *refs):
    fields, (held, before, packed, stats, parts, y) = refs[:-6], refs[-6:]
    readers = [reader(rows, width, *fields[k : k + 2]) for k in range(0, len(fields), 2)]
    for b in range(3):
        for i in range(rows):
            parts[b, i] = taps(readers, held, b, i + 1, before[b, i + 1])
    finish(parts, y, packed, stats, rows, width, per_group)


def conv_edge(rows, width, *refs):
    fields, (held, before, packed, out) = refs[:-4], refs[-4:]
    readers = [reader(rows, width, *fields[k : k + 3]) for k in range(0, len(fields), 3)]
    count = rows * width
    centre = packed[count : count + PAD, :].astype(F32)[:1]
    for j, i in enumerate((0, rows + 1)):
        y = joined_taps(*[taps(readers, held, b, i, before[b, i]) for b in range(3)])
        out[j * width : (j + 1) * width, :] = (y - centre).astype(BF16)


def activated(rows, width, flags, fields, norms, hidden):
    count = rows * width
    for k in range(len(norms)):
        main, edge = fields[2 * k : 2 * k + 2]
        scale = norms[k][0][:1]
        mid = main[count : count + PAD, :].astype(F32)[:1]
        shift = mid * scale + norms[k][1][:1]
        for r in range(rows + 2):
            if r == 0:
                v = edge[0:width, :]
            elif r == rows + 1:
                v = edge[width : 2 * width, :]
            else:
                v = main[(r - 1) * width : r * width, :]
            v = v.astype(F32) * scale + shift
            v = v * (0.5 + 0.5 * jnp.tanh(0.5 * v))
            if r == 0:
                v = jnp.where(flags[0] > 0, v, 0.0)
            if r == rows + 1:
                v = jnp.where(flags[1] > 0, v, 0.0)
            hidden[k, r * width : (r + 1) * width, :] = v.astype(BF16)
    return [
        (lambda r, k=k: hidden[k, r * width : (r + 1) * width, :]) for k in range(len(norms))
    ]


def second_near(rows, width, flags, *refs):
    fields, norms, (held, parts, hidden) = refs[:4], refs[4:6], refs[6:]
    readers = activated(rows, width, flags, fields, norms, hidden)
    for b in range(3):
        for i in range(rows):
            parts[b, i] = taps(readers, held, b, i, None)


def second_far(rows, width, per_group, n, flags, *refs):
    fields, norms = refs[: 2 * n], refs[2 * n : 3 * n]
    held, near, y, packed, stats, parts, hidden = refs[3 * n :]
    held = held.at[2:]
    readers = activated(rows, width, flags, fields, norms, hidden)
    for b in range(3):
        for i in range(rows):
            parts[b, i] = taps(readers, held, b, i, near[b, i])
    finish(parts, y, packed, stats, rows, width, per_group)


def head(count, n, tile, *refs):
    starts, devs, norms = refs[:n], refs[n : 2 * n], refs[2 * n : 3 * n]
    held, ids, out, feat, logits, top, summed, picked = refs[3 * n :]
    step = 256
    tiles = held.shape[2] // tile
    for k in range(n):
        scale = norms[k][0][:1]
        mid = devs[k][count : count + PAD, :].astype(F32)[:1]
        shift = mid * scale + norms[k][1][:1]
        for r in range(0, count, step):
            value = devs[k][r : r + step, :].astype(F32) * scale + shift
            feat[k, r : r + step, :] = (starts[k][r : r + step, :].astype(F32) + value).astype(BF16)
    top[...] = jnp.full(top.shape, -jnp.inf, F32)
    summed[...] = jnp.zeros(summed.shape, F32)
    picked[...] = jnp.zeros(picked.shape, F32)

    def multiply(t, slot):
        total = None
        for k in range(n):
            part = jnp.dot(
                feat[k],
                held[k, :, t * tile : (t + 1) * tile],
                preferred_element_type=F32,
            )
            total = part if total is None else total + part
        logits[slot] = total

    def reduce(t, slot):
        for r in range(0, count, 64):
            rows = slice(r, r + 64)
            pieces = [logits[slot, rows, g : g + 128] for g in range(0, tile, 128)]
            old = top[rows, :]
            new = old
            for piece in pieces:
                new = jnp.maximum(new, piece)
            total = summed[rows, :] * jnp.exp(old - new)
            hit = picked[rows, :]
            rel = ids[rows, :] - t * tile
            for g, piece in enumerate(pieces):
                total = total + jnp.exp(piece - new)
                hit = jnp.where(rel == g * 128, piece, hit)
            top[rows, :] = new
            summed[rows, :] = total
            picked[rows, :] = hit

    for t in range(tiles):
        multiply(t, t % 2)
        reduce(t, t % 2)
    lane = lax.broadcasted_iota(jnp.int32, (128, 128), 1)
    for r in range(0, count, 128):
        rows = slice(r, r + 128)
        high = jnp.max(top[rows, :], axis=1, keepdims=True)
        total = jnp.sum(summed[rows, :] * jnp.exp(top[rows, :] - high), axis=1, keepdims=True)
        hit = jnp.sum(picked[rows, :], axis=1, keepdims=True)
        stacked = jnp.where(lane == 0, high, jnp.where(lane == 1, total, hit))
        out[:, rows] = jnp.transpose(stacked)[:8]


def in_hbm(value):
    return pltpu.with_memory_space_constraint(value, pltpu.HBM)


def params(mib):
    return pltpu.CompilerParams(vmem_limit_bytes=mib << 20)


def over_rows(stats, count, per_group, gains, biases, between=None):
    stats = jnp.stack([stats] + cross(stats))
    population = float(count * per_group)
    n = lax.axis_size("rows")
    step = 1
    while step < n:
        radix = 4 if step > 1 and n // step % 4 == 0 else 2
        others = []
        for j in range(1, radix):
            move = [(i, i ^ (step * j)) for i in range(n)]
            others.append(lax.ppermute(stats, "rows", move))
        states = [stats] + others
        mid = sum(t[:, 0] for t in states) / radix
        away = sum((t[:, 0] - mid) * (t[:, 0] - mid) for t in states)
        stats = jnp.stack([mid, sum(t[:, 1] for t in states) + population * away], axis=1)
        population *= radix
        step *= radix
        if between is not None:
            between(stats)
            between = None
    scale = gains / jnp.sqrt(stats[:, 1] / population + EPS)
    mine = jnp.stack([scale, biases - stats[:, 0] * scale], axis=1)
    other = swap(mine)
    return [f for k in range(mine.shape[0]) for f in (mine[k], other[k])]


def step_of(
    token_ids,
    keep_mask,
    remask_order,
    embed_table,
    mask_embed,
    conv_one,
    gain_one,
    bias_one,
    conv_two,
    gain_two,
    bias_two,
    head_weight,
):
    rows, width = token_ids.shape
    n_rows = lax.axis_size("rows")
    n = lax.axis_size("cols")
    height = rows * n_rows
    here = gain_one.shape[0]
    per_group = here * n // GROUPS
    count = rows * width
    me_row = lax.axis_index("rows")
    flags = jnp.stack([me_row > 0, me_row < n_rows - 1]).astype(jnp.int32)
    src = jnp.stack(sources()).astype(jnp.int32)

    def look(codes):
        rows_of = jnp.take(embed_table, jnp.maximum(codes - 2, 0), axis=0, mode="clip")
        rows_of = jnp.where(codes[:, None] == 1, mask_embed[None, :], rows_of)
        return jnp.where(codes[:, None] == 0, 0, rows_of)

    looked = jnp.take(embed_table, token_ids.reshape(-1), axis=0, mode="clip")
    main_far = cross(looked)
    token_ids, keep_mask, remask_order, looked = lax.optimization_barrier(
        (token_ids, keep_mask, remask_order, looked)
    )
    visible = (keep_mask.reshape(-1) == 1) | (remask_order >= height * width // 2)
    code = jnp.where(visible, token_ids.reshape(-1) + 2, 1)
    start = jnp.where(visible[:, None], looked, mask_embed[None, :])
    above, below = upward(code[count - 2 * width :]), downward(code[: 2 * width])
    halo = look(
        jnp.concatenate([above[width:], below[:width], above[:width], below[width:]])
    )
    inner, outer = halo[: 2 * width], halo[2 * width :]
    mains = [start, swap(start)]
    inners, inner_far = [inner, swap(inner)], cross(inner)
    outers, outer_far = [outer, swap(outer)], cross(outer)

    packed_shape = jax.ShapeDtypeStruct((count + PAD, here), BF16)
    stats_shape = jax.ShapeDtypeStruct((2, 8, here), F32)
    parts_shape = (3, rows, width, here)
    y_shape = (count, here)
    own = jnp.stack([gain_one, bias_one, gain_two, bias_two, mask_embed.astype(F32)])
    own = jnp.broadcast_to(own[:, None], (5, 8, here))
    affine = jnp.stack([own] + cross(own))
    mask_far = affine[1:, 4, 0].astype(BF16)
    main_far = [
        jnp.where(visible[:, None], far, mask_far[k]) for k, far in enumerate(main_far)
    ]
    fields = [f for k in range(2) for f in (mains[k], inners[k], outers[k])]
    vocab_here = head_weight.shape[1]
    near, taps_far = pl.pallas_call(
        lambda *refs: conv_near(rows, width, *refs),
        out_shape=(
            jax.ShapeDtypeStruct((3, rows + 2, width, here), F32),
            jax.ShapeDtypeStruct((n - 2, 3, 3, here, here), BF16),
        ),
        in_specs=[SMEM] + [VMEM] * 6 + [HBM],
        out_specs=(VMEM,) * 2,
        scratch_shapes=[
            pltpu.VMEM((2, 3, 3, here, here), BF16),
            pltpu.SemaphoreType.DMA((3, 2)),
            pltpu.SemaphoreType.DMA((3, n - 2)),
        ],
        compiler_params=params(12),
        name="conv_near",
    )(src, *fields, in_hbm(conv_one))
    mains += far_blocks(main_far, near)
    inners += far_blocks(inner_far, near)
    outers += far_blocks(outer_far, near)
    fields = [f for k in range(2, n) for f in (mains[k], inners[k])]
    packed, stats = pl.pallas_call(
        lambda *refs: conv_far(rows, width, per_group, *refs),
        out_shape=(packed_shape, stats_shape),
        in_specs=[VMEM] * (len(fields) + 2),
        out_specs=(VMEM, VMEM),
        scratch_shapes=[pltpu.VMEM(parts_shape, F32), pltpu.VMEM(y_shape, F32)],
        compiler_params=params(12),
        name="conv_far",
    )(*fields, taps_far, near)
    fields = [f for k in range(2, n) for f in (mains[k], inners[k], outers[k])]
    edge_box = []

    def make_edge(state):
        centre, _ = lax.optimization_barrier((packed, state))
        edge_box.append(
            pl.pallas_call(
                lambda *refs: conv_edge(rows, width, *refs),
                out_shape=jax.ShapeDtypeStruct((2 * width, here), BF16),
                in_specs=[VMEM] * (len(fields) + 3),
                out_specs=VMEM,
                compiler_params=params(8),
                name="conv_edge",
            )(*fields, taps_far, near, centre)
        )

    norms = over_rows(stats, count, per_group, affine[:, 0], affine[:, 1], make_edge)
    blocks = gathered(packed, norms[0])
    edges = gathered(edge_box[0], norms[0])
    fields = [f for two in zip(blocks, edges) for f in two]
    when, _ = lax.optimization_barrier((src, edge_box[0]))
    taps_two = pl.pallas_call(
        fetch_taps,
        out_shape=jax.ShapeDtypeStruct((n, 3, 3, here, here), BF16),
        in_specs=[SMEM, HBM],
        out_specs=VMEM,
        scratch_shapes=[pltpu.SemaphoreType.DMA((3, n))],
        compiler_params=params(8),
        name="fetch_two",
    )(when, in_hbm(conv_two))
    near = pl.pallas_call(
        lambda *refs: second_near(rows, width, *refs),
        out_shape=jax.ShapeDtypeStruct(parts_shape, F32),
        in_specs=[SMEM] + [VMEM] * 7,
        out_specs=VMEM,
        scratch_shapes=[pltpu.VMEM((2, count + 2 * width, here), BF16)],
        compiler_params=params(12),
        name="two_near",
    )(flags, *fields[:4], *norms[:2], taps_two)
    fields = fields[:4] + list(
        lax.optimization_barrier((near, *fields[4:]))
    )
    near = fields.pop(4)
    y_two, packed, stats = pl.pallas_call(
        lambda *refs: second_far(rows, width, per_group, n - 2, *refs),
        out_shape=(jax.ShapeDtypeStruct(y_shape, F32), packed_shape, stats_shape),
        in_specs=[SMEM] + [VMEM] * (3 * (n - 2) + 2),
        out_specs=(VMEM, VMEM, VMEM),
        scratch_shapes=[
            pltpu.VMEM(parts_shape, F32),
            pltpu.VMEM((n - 2, count + 2 * width, here), BF16),
        ],
        compiler_params=params(12),
        name="two_far",
    )(flags, *fields[4:], *norms[2:], taps_two, near)

    norms = over_rows(stats, count, per_group, affine[:, 2], affine[:, 3])
    blocks = gathered(packed, norms[0])
    when, _ = lax.optimization_barrier((src, packed))
    head_in = pl.pallas_call(
        fetch_head,
        out_shape=jax.ShapeDtypeStruct((n, here, vocab_here), BF16),
        in_specs=[SMEM, HBM],
        out_specs=VMEM,
        scratch_shapes=[pltpu.SemaphoreType.DMA((n,))],
        compiler_params=params(8),
        name="fetch_head",
    )(when, in_hbm(head_weight))
    features = start.astype(F32) + (y_two * norms[0][0, :1] + norms[0][1, :1])
    features = features.astype(BF16).reshape(rows, width, here)

    ids = token_ids.reshape(-1, 1) - lax.axis_index("cols") * vocab_here
    ids = ids - lax.broadcasted_iota(jnp.int32, (1, 128), 1)
    ids, features = lax.optimization_barrier((ids, features))
    tile = min(512, vocab_here)
    state = pl.pallas_call(
        lambda *refs: head(count, n, tile, *refs),
        out_shape=jax.ShapeDtypeStruct((8, count), F32),
        in_specs=[VMEM] * (3 * n + 2),
        out_specs=VMEM,
        scratch_shapes=[
            pltpu.VMEM((n, count, here), BF16),
            pltpu.VMEM((2, count, tile), F32),
            pltpu.VMEM((count, 128), F32),
            pltpu.VMEM((count, 128), F32),
            pltpu.VMEM((count, 128), F32),
        ],
        compiler_params=params(16),
        name="head",
    )(*mains, *blocks, *norms, head_in, ids)
    states = [state] + [
        lax.ppermute(state, "cols", [(i, i ^ k) for i in range(n)]) for k in range(n - 1, 0, -1)
    ]
    high = states[0][0]
    for other in states[1:]:
        high = jnp.maximum(high, other[0])
    total = sum(t[1] * jnp.exp(t[0] - high) for t in states)
    state = (high, total, sum(t[2] for t in states))
    logp = (state[2] - state[0] - jnp.log(state[1])).reshape(rows, width)
    slice_width = width // n
    token_logp = lax.dynamic_slice_in_dim(
        logp, lax.axis_index("cols") * slice_width, slice_width, 1
    )
    return (features, token_logp)


def solution(mesh):
    in_specs = (
        P("rows", None),
        P("rows", None),
        P("rows"),
        P(None, "cols"),
        P("cols"),
        P(None, None, None, "cols"),
        P("cols"),
        P("cols"),
        P(None, None, None, "cols"),
        P("cols"),
        P("cols"),
        P(None, "cols"),
    )
    out_specs = (P("rows", None, "cols"), P("rows", "cols"))
    return jax.shard_map(step_of, mesh=mesh, in_specs=in_specs, out_specs=out_specs, check_vma=False)
```
